32 devices in a mesh: brain: 2 (over x), slab: 16 (over z, y, core).
Axes of the slice: x: 2, y: 2, z: 4, core: 2. Of those that a mesh axis runs over, the one named last changes fastest.
Arguments:
- features: bfloat16 [32, 192, 16, 128], P(None, ('brain', 'slab')), parts along dimension 1, may hold values from -6 to 6
- conv_weight: bfloat16 [3, 128, 288], replicated, may hold values from -0.21875 to 0.21875
- norm_gain: float32 [4, 32], replicated, may hold values from 0.25 to 1.75
- norm_bias: float32 [4, 32], replicated, may hold values from -3 to 3
- head_weight: bfloat16 [4, 6, 32], replicated, may hold values from -2 to 2
- head_bias: float32 [4, 6], replicated, may hold values from -4 to 308
- patch_offsets: int32 [32, 2], P(('brain', 'slab')), parts along dimension 0, may hold values from -2 to 2
- fg_mask: int32 [32, 2], P(('brain', 'slab')), parts along dimension 0, may hold values 0 or 1
- acq_counts: int32 [32], P(('brain', 'slab')), parts along dimension 0, may hold values from 1 to 8, 64 in all
Outputs:
- resampled: float32 [6, 256, 16, 128], P(None, ('brain', 'slab')), parts along dimension 1
The draws below stay inside these ranges and needn't reach their ends.
There are 2 independent parts, one for each index of `brain`. The reference program is written for one: setup_inputs(seed, part) draws one part's arguments, and reference() takes and returns one part's arrays. A program takes and returns all parts, laid end to end along the dimension named above; an argument that names none is the same for every part. Nothing has to cross between parts.
Inputs may be any that keep to these rules, and one draw needn't show every extreme that they name: `acq_counts`: within each brain volume separately, the 16 counts of that volume sum to 64 and some slab of that volume has exactly 8; the array of all volumes together sums to 64 once for every volume.
All inputs are finite; a program needn't handle non-finite values. No bound on the sum of `fg_mask` or of `acq_counts` on one device may be relied on, other than what follows from the above.
Results may differ from the reference program's by a relative error of at most 0.0003.
Values may be sent and summed in bfloat16 or wider, within the bound.
No kernel may reach another device: no remote copies, remote signals or barrier semaphores. Data moves between devices by JAX's collectives and lax.ppermute only.
A program may use at most 64 MiB of HBM per device.

```python
import math
import jax
import jax.numpy as jnp
import numpy as np
from jax import lax

CHANNELS = 32
CLASSES = 6
FOLDS = 4
SLAB_X = 6
MARGIN = 2
JITTER = 2
PATCHES = 2
PATCH_ROWS = 8
COLUMNS = 128
RIM = 4
PATCH_X = 10
ROWS = 16
SLABS = 16
VOLUME_X = 96
ACQ_DEV = 4
MOST_ACQ = 8


def draw_head_bias(key, part):
    biases = jnp.clip(jax.random.normal(key, (FOLDS, CLASSES), jnp.float32), -4.0, 4.0)
    return biases


def with_ends(result, rng, least, top_value):
    dims = result.shape
    place = [jax.random.randint(jax.random.fold_in(rng, axis), (), 0, dims[axis]) for axis in range(len(dims))]
    result = result.at[tuple(place)].set(least)
    longest = dims.index(max(dims))
    place[longest] = (place[longest] + 1) % dims[longest]
    return result.at[tuple(place)].set(top_value)


def levels(key, dims, cuts, smallest, largest):
    factor_of = 1.0
    for position, shards_of in cuts:
        draws = jax.random.uniform(jax.random.fold_in(jax.random.fold_in(key, 6), position), (shards_of,), jnp.float32, smallest / len(cuts), largest / len(cuts))
        factor_of = factor_of * jnp.repeat(jnp.exp(draws), dims[position] // shards_of).reshape((-1,) + (1,) * (len(dims) - 1 - position))
    return factor_of


def profile(amount, total, most, slope):
    weights = [(1 << 20) // math.isqrt(grade ** slope) + 1 for grade in range(2, amount + 1)]
    spare, given = total - most - (amount - 1), [1] * (amount - 1)
    while spare > 0:
        free = [i for i in range(amount - 1) if given[i] < most]
        pool, remaining = sum([weights[i] for i in free]), spare
        for i in free:
            addition = min(most - given[i], max(1, remaining * weights[i] // pool), spare)
            given[i] = given[i] + addition
            spare = spare - addition
    return np.array([most] + given)


def uneven(rng, amount, total, most, skew):
    if amount == 2:
        one = jax.random.randint(rng, (), max(1, total - most), min(most, total - 1) + 1)
        return jnp.stack([one, total - one])
    lengths = jnp.asarray(profile(amount, total, most, skew), jnp.int32)
    couples = (amount - 1) // 2
    source_of, sink = lengths[1:1 + 2 * couples:2], lengths[2:2 + 2 * couples:2]
    margin = jnp.minimum(source_of - 1, most - sink)
    passed = jax.random.randint(jax.random.fold_in(rng, 1), (couples,), 0, 1 << 20) % (margin + 1)
    lengths = lengths.at[1:1 + 2 * couples:2].set(source_of - passed).at[2:2 + 2 * couples:2].set(sink + passed)
    return lengths[jax.random.permutation(jax.random.fold_in(rng, 2), amount)]


def gaussian(stream_key, shape, scale, bound, cuts=(), kind=jnp.bfloat16):
    level = levels(stream_key, shape, cuts, -0.22, 0.18) if cuts else 1.0
    result = jax.random.normal(stream_key, shape, jnp.float32) * scale * level
    return jnp.minimum(jnp.maximum(result, -bound), bound).astype(kind)


def setup_inputs(seed: int = 0, part: int = 0) -> dict:
    key_list = jax.random.split(jax.random.key(seed), 10)
    part_splits = jax.random.split(jax.random.fold_in(key_list[9], part), 10)
    return {
        "features": gaussian(part_splits[0], (CHANNELS, VOLUME_X, ROWS, COLUMNS), 1.0, 6.0, ((1, 16),)),
        "conv_weight": gaussian(key_list[1], (3, FOLDS * CHANNELS, 9 * CHANNELS), (27 * CHANNELS) ** -0.5, 0.21875),
        "norm_gain": jnp.clip(1.0 + 0.15 * jax.random.normal(key_list[2], (FOLDS, CHANNELS), jnp.float32), 0.25, 1.75),
        "norm_bias": gaussian(key_list[3], (FOLDS, CHANNELS), 0.7, 3.0, (), jnp.float32),
        "head_weight": gaussian(key_list[4], (FOLDS, CLASSES, CHANNELS), (CHANNELS // 4) ** -0.5, 2.0),
        "head_bias": draw_head_bias(jax.random.fold_in(key_list[9], 71), part),
        "patch_offsets": with_ends(jax.random.randint(part_splits[6], (SLABS, PATCHES), 0 - JITTER, JITTER + 1), jax.random.fold_in(part_splits[6], 1), 0 - JITTER, JITTER).astype(jnp.int32),
        "fg_mask": with_ends((jax.random.randint(part_splits[7], (SLABS, PATCHES), 0, 4) < 3).astype(jnp.int32), jax.random.fold_in(part_splits[7], 1), 0, 1),
        "acq_counts": uneven(part_splits[8], SLABS, ACQ_DEV * SLABS, MOST_ACQ, 1).astype(jnp.int32),
    }


prior_weight = 0.1

def gauss_line(length):
    positions = jnp.arange(length, dtype=jnp.float32)
    centre = (length - 1) / 2.0
    spread = length / 4.0
    scaled = (positions - centre) / spread
    return jnp.exp(-0.5 * scaled * scaled)

def patch_scores(patch, conv_weight, norm_gain, norm_bias, head_weight, head_bias):
    channels, length, row_span, column_count = patch.shape
    padded = jnp.pad(patch, ((0, 0), (1, 1), (1, 1), (0, 0)))
    zero_col = jnp.zeros(padded.shape[:-1] + (1,), padded.dtype)
    shifted = (jnp.concatenate([zero_col, padded[..., :-1]], -1), padded, jnp.concatenate([padded[..., 1:], zero_col], -1))
    tap_list = [source[:, :, row_shift:row_shift + row_span] for row_shift in range(3) for source in shifted]
    stacked = jnp.concatenate(tap_list, 0)
    conv_out = jnp.zeros((conv_weight.shape[1], length * row_span * column_count), jnp.float32)
    for depth_tap in range(3):
        sliced = stacked[:, depth_tap:depth_tap + length].reshape(9 * channels, -1)
        conv_out = conv_out + jnp.dot(conv_weight[depth_tap], sliced, preferred_element_type=jnp.float32)
    centre_mean = lax.optimization_barrier(jnp.mean(conv_out, axis=1, keepdims=True))
    centred = conv_out - centre_mean
    variance = lax.optimization_barrier(jnp.mean(centred * centred, axis=1, keepdims=True))
    normed = centred * lax.rsqrt(variance + 1e-05) * norm_gain.reshape(-1)[:, None] + norm_bias.reshape(-1)[:, None]
    activated = jnp.where(normed > 0, normed, 0.01 * normed)
    fold_count = head_weight.shape[0]
    logits = jnp.einsum('fkc,fcv->fkv', head_weight.astype(jnp.float32), activated.reshape(fold_count, channels, -1).astype(jnp.float32), precision=lax.Precision.HIGHEST) + head_bias[:, :, None]
    class_probs = lax.optimization_barrier(jnp.sum(jax.nn.softmax(logits, axis=1), axis=0)) / fold_count
    window = (gauss_line(length)[:, None, None] * gauss_line(row_span)[None, :, None] * gauss_line(column_count)[None, None, :]).reshape(-1)
    weighted = (class_probs * window[None, :]).reshape(-1, length, row_span, column_count)
    return (weighted, window.reshape(length, row_span, column_count))

def reference(features, conv_weight, norm_gain, norm_bias, head_weight, head_bias, patch_offsets, fg_mask, acq_counts):
    channels, volume, row_total, column_count = features.shape
    padded = jnp.pad(features, ((0, 0), (RIM, RIM), (0, 0), (0, 0)))
    prob_init = jnp.zeros((CLASSES, volume + 2 * RIM, row_total, column_count), jnp.float32)
    weight_init = jnp.zeros((volume + 2 * RIM, row_total, column_count), jnp.float32)
    zero_index = jnp.zeros((), jnp.int32)

    def one_slab(carry, slab_id):
        prob_sums, weight_sums = carry
        for patch_index in range(PATCHES):
            row_first = patch_index * PATCH_ROWS
            row_index = jnp.asarray(row_first, jnp.int32)
            patch_start = (slab_id * SLAB_X + RIM - MARGIN + patch_offsets[slab_id, patch_index]).astype(jnp.int32)
            patch = lax.dynamic_slice_in_dim(padded[:, :, row_first:row_first + PATCH_ROWS], patch_start, PATCH_X, 1)
            class_probs, window = patch_scores(patch, conv_weight, norm_gain, norm_bias, head_weight, head_bias)
            keep_value = fg_mask[slab_id, patch_index].astype(jnp.float32)
            old_probs = lax.dynamic_slice(prob_sums, (zero_index, patch_start, row_index, zero_index), class_probs.shape)
            prob_sums = lax.dynamic_update_slice(prob_sums, old_probs + class_probs * keep_value, (zero_index, patch_start, row_index, zero_index))
            old_weights = lax.dynamic_slice(weight_sums, (patch_start, row_index, zero_index), window.shape)
            weight_sums = lax.dynamic_update_slice(weight_sums, old_weights + window * keep_value, (patch_start, row_index, zero_index))
        return ((prob_sums, weight_sums), None)
    (prob_sums, weight_sums), unused = lax.scan(one_slab, (prob_init, weight_init), jnp.arange(SLABS, dtype=jnp.int32))
    background = (jnp.arange(CLASSES) == 0).astype(jnp.float32)[:, None, None, None] * prior_weight
    merged = (prob_sums[:, RIM:RIM + volume] + background) / (weight_sums[RIM:RIM + volume] + prior_weight)
    edged = jnp.pad(merged, ((0, 0), (1, 1), (0, 0), (0, 0)))

    def resample(slab_id):
        acq_count = acq_counts[slab_id].astype(jnp.float32)
        slot_ids = jnp.arange(MOST_ACQ, dtype=jnp.float32)
        step_size = SLAB_X / jnp.maximum(acq_count - 1.0, 1.0)
        local_pos = slot_ids * step_size - 0.5
        slab_anchor = (slab_id * SLAB_X).astype(jnp.float32)
        global_pos = jnp.clip(slab_anchor + local_pos, 0.0, float(volume - 1))
        local_pos = global_pos - slab_anchor
        plane_pos = jnp.arange(SLAB_X + 2, dtype=jnp.float32) - 1.0
        used = (slot_ids < acq_count).astype(jnp.float32)
        resample_matrix = jnp.maximum(0.0, 1.0 - jnp.abs(local_pos[:, None] - plane_pos[None, :])) * used[:, None]
        planes_near = lax.dynamic_slice_in_dim(edged, (slab_id * SLAB_X).astype(jnp.int32), SLAB_X + 2, 1)
        return jnp.einsum('kj,cjhw->ckhw', resample_matrix, planes_near, precision=lax.Precision.HIGHEST)
    stacked = lax.map(resample, jnp.arange(SLABS, dtype=jnp.int32))
    return jnp.transpose(stacked, (1, 0, 2, 3, 4)).reshape(CLASSES, SLABS * MOST_ACQ, row_total, column_count)
```

```python
import functools
import jax
import jax.numpy as jnp
from jax import lax
from jax.experimental import pallas as pl
from jax.experimental.pallas import tpu as pltpu
from jax.sharding import PartitionSpec as P

PATCHES = 2
PATCH_ROWS = 8
MARGIN = 2
RIM = 4
PATCH_X = 10
MOST_ACQ = 8
PRIOR = 0.1
EPS = 1e-05
F32 = jnp.float32
BF16 = jnp.bfloat16
MIB = 1 << 20


def vmem():
    return pl.BlockSpec(memory_space=pltpu.VMEM)


def smem():
    return pl.BlockSpec(memory_space=pltpu.SMEM)


def prep_kernel(feat, own, to_a, to_b):
    channels, planes, rows, cols = feat.shape
    even = lax.rem(lax.axis_index("slab"), 2) == 0
    a_first = jnp.where(even, planes - RIM, 0)
    b_first = jnp.where(even, 0, planes - RIM)
    for x in range(planes):
        turned = jnp.swapaxes(feat[:, x].astype(F32), 0, 1).astype(BF16)
        own[x] = turned.reshape(own.shape[1:])
    to_a[...] = own[pl.ds(a_first, RIM)]
    to_b[...] = own[pl.ds(b_first, RIM)]


def column_of(table, folds, width):
    diag = lax.broadcasted_iota(jnp.int32, (width, width), 0) == lax.broadcasted_iota(jnp.int32, (width, width), 1)
    parts = []
    for f in range(folds):
        row = jnp.broadcast_to(table[f : f + 1, :], (width, width))
        parts.append(jnp.sum(jnp.where(diag, row, 0.0), axis=1, keepdims=True))
    return jnp.concatenate(parts, 0)


def head_tables(head_w, head_b, folds, classes, channels):
    rows = classes * 2 * folds
    row = lax.broadcasted_iota(jnp.int32, (rows, classes), 0)
    cls = lax.broadcasted_iota(jnp.int32, (rows, classes), 1)
    brow = lax.broadcasted_iota(jnp.int32, (rows, classes), 0)
    lane = lax.broadcasted_iota(jnp.int32, (channels, folds * channels), 1)
    chan = lax.broadcasted_iota(jnp.int32, (channels, folds * channels), 0)
    table = jnp.zeros((rows, folds * channels), F32)
    bias = jnp.zeros((rows, 1), F32)
    for f in range(folds):
        pick = (row // (2 * folds) == cls) & (row % folds == f)
        part = jnp.dot(pick.astype(F32).astype(BF16), head_w[f], preferred_element_type=F32).astype(BF16)
        place = (lane == chan + f * channels).astype(F32).astype(BF16)
        table = table + jnp.dot(part, place, preferred_element_type=F32)
        bias = bias + jnp.sum(jnp.where(pick, jnp.broadcast_to(head_b[f : f + 1, :], (rows, classes)), 0.0), axis=1, keepdims=True)
    table = table.astype(BF16)
    return jnp.concatenate([table, table], 1), bias


def gauss(position, length):
    scaled = (position - (length - 1) / 2.0) / (length / 4.0)
    return jnp.exp(-0.5 * scaled * scaled)


def fill_taps(taps, plane, source):
    rows, channels, cols = source.shape
    lane = lax.broadcasted_iota(jnp.int32, (channels, cols), 1)
    for h in range(rows):
        value = source[h]
        wide = value.astype(F32)
        left = jnp.where(lane == 0, 0.0, pltpu.roll(wide, 1, 1)).astype(BF16)
        right = jnp.where(lane == cols - 1, 0.0, pltpu.roll(wide, cols - 1, 1)).astype(BF16)
        taps[plane, h + 1] = jnp.concatenate([left, value, right], 0)


def main_kernel(offs, mask, own, from_a, from_b, wt, gain, nbias, head_w, head_b, kept, to_a, to_b, taps, w_all, conv, placed, shift, sums, squares):
    planes = own.shape[0]
    folds, classes, channels = head_w.shape
    outs = folds * channels
    cols = own.shape[-1]
    span = planes + 2 * RIM
    zero_plane = span
    even = lax.rem(lax.axis_index("slab"), 2) == 0
    a_base = jnp.where(even, RIM + planes, 0)
    b_base = jnp.where(even, 0, RIM + planes)
    wide_w = jnp.concatenate([wt[a].astype(F32) for a in range(3)], 0)
    w_all[...] = jnp.transpose(wide_w).astype(BF16)
    head, hbias = head_tables(head_w, head_b, folds, classes, channels)
    hbias = jnp.broadcast_to(hbias, (classes * 2 * folds, 2 * cols))
    gain_col = column_of(gain, folds, channels)
    bias_col = column_of(nbias, folds, channels)
    zero_row = jnp.zeros((3 * channels, cols), BF16)
    taps[zero_plane] = jnp.zeros(taps.shape[1:], BF16)
    sub = lax.broadcasted_iota(jnp.int32, (2 * folds, cols), 0)
    lane = lax.broadcasted_iota(jnp.int32, (2 * folds, cols), 1)
    line = gauss(sub.astype(F32), PATCH_ROWS) * gauss(lane.astype(F32), cols)
    for p in range(PATCHES):
        first = RIM - MARGIN + offs[0, p]

        def pad_rows(i, _):
            taps[i, 0] = zero_row
            taps[i, PATCH_ROWS + 1] = zero_row
            return 0

        lax.fori_loop(0, span, pad_rows, 0)

        def fill_own(i, _):
            fill_taps(taps, i + RIM, own.at[i, p])
            return 0

        def fill_rim(i, _):
            fill_taps(taps, i + a_base, from_a.at[i, p])
            fill_taps(taps, i + b_base, from_b.at[i, p])
            return 0

        lax.fori_loop(0, planes, fill_own, 0)
        lax.fori_loop(0, RIM, fill_rim, 0)
        sums[...] = jnp.zeros_like(sums)
        squares[...] = jnp.zeros_like(squares)

        def conv_plane(x, _):
            i = first + x
            below = jnp.where(x == 0, zero_plane, i - 1)
            above = jnp.where(x == PATCH_X - 1, zero_plane, i + 1)
            weights = w_all[...]
            for r in range(PATCH_ROWS // 2):
                halves = []
                for h in (r, r + PATCH_ROWS // 2):
                    halves.append(jnp.concatenate([taps[t, h : h + 3].reshape(9 * channels, cols) for t in (below, i, above)], 0))
                out = jnp.dot(weights, jnp.concatenate(halves, 1), preferred_element_type=F32)
                conv[x, r] = out
                one, two = out[:, :cols], out[:, cols:]
                if r == 0:
                    @pl.when(x == 0)
                    def _():
                        shift[...] = 0.5 * (one + two)
                base = shift[...]
                one, two = one - base, two - base
                sums[...] += one + two
                squares[...] += one * one + two * two
            return 0

        lax.fori_loop(0, PATCH_X, conv_plane, 0)
        count = float(PATCH_X * PATCH_ROWS)
        total = sums[...] * (1.0 / count)
        spread = squares[...] - total * sums[...]
        lane_mean = shift[...] + total
        mean = jnp.mean(lane_mean, axis=1, keepdims=True)
        dev = lane_mean - mean
        var = jnp.sum(spread + count * dev * dev, axis=1, keepdims=True) * (1.0 / (count * cols))
        scale = lax.rsqrt(var + EPS) * gain_col
        scale_b = jnp.broadcast_to(scale, (outs, 2 * cols))
        offset_b = jnp.broadcast_to(bias_col - mean * scale, (outs, 2 * cols))
        keep = mask[0, p].astype(F32) * 0.25
        placed[...] = jnp.zeros_like(placed)

        def finish_plane(x, _):
            lower = sub < folds
            table = [[] for _ in range(classes)]
            for r in range(PATCH_ROWS // 2):
                act = conv[x, r] * scale_b + offset_b
                act = jnp.maximum(act, 0.01 * act)
                high = act.astype(BF16)
                low = (act - high.astype(F32)).astype(BF16)
                logits = jnp.dot(head, jnp.concatenate([high, low], 0), preferred_element_type=F32) + hbias
                parts = []
                for k in range(classes):
                    both = logits[k * 2 * folds : (k + 1) * 2 * folds]
                    parts.append(jnp.where(lower, both[:, :cols], both[:, cols:]))
                top = functools.reduce(jnp.maximum, parts)
                parts = [jnp.exp(v - top) for v in parts]
                denom = 1.0 / functools.reduce(jnp.add, parts)
                for k in range(classes):
                    table[k].append(parts[k] * denom)
            window = line * (gauss(jnp.full((2 * folds, cols), x, jnp.int32).astype(F32), PATCH_X) * keep)
            for k in range(classes):
                v = table[k]
                odd = (sub % 2) == 1
                high_pair = (sub % 4) >= 2
                pairs = []
                for q in (0, 2):
                    pairs.append(jnp.where(odd, v[q + 1] + pltpu.roll(v[q + 1], 1, 0), v[q] + pltpu.roll(v[q], 7, 0)))
                full = jnp.where(high_pair, pairs[1] + pltpu.roll(pairs[1], 2, 0), pairs[0] + pltpu.roll(pairs[0], 6, 0))
                placed[first + x, k] = full * window
            return 0

        lax.fori_loop(0, PATCH_X, finish_plane, 0)
        reach = RIM + 1
        kept[p] = placed[pl.ds(RIM - 1, planes + 2)]
        a_first = jnp.where(even, planes + RIM - 1, 0)
        b_first = jnp.where(even, 0, planes + RIM - 1)
        to_a[p] = placed[pl.ds(a_first, reach)]
        to_b[p] = placed[pl.ds(b_first, reach)]


def merge_kernel(slabs, acq, kept, from_a, from_b, out, merged):
    wide = kept.shape[1]
    planes = wide - 2
    classes = kept.shape[2]
    rows, cols = kept.shape[3:]
    slab = lax.axis_index("slab")
    even = lax.rem(slab, 2) == 0
    a_base = jnp.where(even, wide - RIM - 1, 0)
    b_base = jnp.where(even, 0, wide - RIM - 1)
    shape = (rows, cols)
    count = jnp.full(shape, acq[0], jnp.int32).astype(F32)
    anchor = jnp.full(shape, slab * planes, jnp.int32).astype(F32)
    step = planes / jnp.maximum(count - 1.0, 1.0)
    for p in range(PATCHES):
        merged[...] = kept[p]
        merged[pl.ds(a_base, RIM + 1)] += from_a[p]
        merged[pl.ds(b_base, RIM + 1)] += from_b[p]
        table = []
        for j in range(wide):
            parts = [merged[j, k] for k in range(classes)]
            scale = 1.0 / (functools.reduce(jnp.add, parts) + PRIOR)
            parts[0] = parts[0] + PRIOR
            table.append([v * scale for v in parts])
        for s in range(MOST_ACQ):
            place = jnp.clip(anchor + (s * step - 0.5), 0.0, float(slabs * planes - 1)) - anchor
            used = (s < count).astype(F32)
            gains = [jnp.maximum(0.0, 1.0 - jnp.abs(place - (j - 1.0))) * used for j in range(wide)]
            for k in range(classes):
                out[k, s, p * rows : (p + 1) * rows] = functools.reduce(jnp.add, [gains[j] * table[j][k] for j in range(wide)])


def local(slabs, features, conv_weight, norm_gain, norm_bias, head_weight, head_bias, patch_offsets, fg_mask, acq_counts):
    channels, planes, row_total, cols = features.shape
    folds, classes, _ = head_weight.shape
    outs = folds * channels
    pairs_a = [(i, i ^ 1) for i in range(slabs) if (i ^ 1) < slabs]
    pairs_b = [(i, ((i + 1) ^ 1) - 1) for i in range(slabs) if 0 <= ((i + 1) ^ 1) - 1 < slabs]
    cell = (PATCHES, PATCH_ROWS, channels, cols)
    params = pltpu.CompilerParams(vmem_limit_bytes=40 * MIB)
    own, to_a, to_b = pl.pallas_call(
        prep_kernel,
        out_shape=[jax.ShapeDtypeStruct((n,) + cell, BF16) for n in (planes, RIM, RIM)],
        in_specs=[vmem()],
        out_specs=[vmem()] * 3,
        compiler_params=params,
        name="prep",
    )(features)
    from_b = lax.ppermute(to_b, "slab", pairs_b)
    from_a = lax.ppermute(to_a, "slab", pairs_a)
    wide = planes + 2
    tile = (classes, PATCH_ROWS, cols)
    span = planes + 2 * RIM
    kept, send_a, send_b = pl.pallas_call(
        main_kernel,
        out_shape=[jax.ShapeDtypeStruct((PATCHES, n) + tile, F32) for n in (wide, RIM + 1, RIM + 1)],
        in_specs=[smem()] * 2 + [vmem()] * 8,
        out_specs=[vmem()] * 3,
        scratch_shapes=[
            pltpu.VMEM((span + 1, PATCH_ROWS + 2, 3 * channels, cols), BF16),
            pltpu.VMEM((outs, 27 * channels), BF16),
            pltpu.VMEM((PATCH_X, PATCH_ROWS // 2, outs, 2 * cols), F32),
            pltpu.VMEM((span,) + tile, F32),
            pltpu.VMEM((outs, cols), F32),
            pltpu.VMEM((outs, cols), F32),
            pltpu.VMEM((outs, cols), F32),
        ],
        compiler_params=params,
        name="main",
    )(patch_offsets, fg_mask, own, from_a, from_b, jnp.swapaxes(conv_weight, 1, 2), norm_gain, norm_bias, head_weight, head_bias)
    got_b = lax.ppermute(send_b, "slab", pairs_b)
    got_a = lax.ppermute(send_a, "slab", pairs_a)
    return pl.pallas_call(
        functools.partial(merge_kernel, slabs),
        out_shape=jax.ShapeDtypeStruct((classes, MOST_ACQ, row_total, cols), F32),
        in_specs=[smem()] + [vmem()] * 3,
        out_specs=vmem(),
        scratch_shapes=[pltpu.VMEM((wide,) + tile, F32)],
        compiler_params=params,
        name="merge",
    )(acq_counts, kept, got_a, got_b)


def solution(mesh):
    part = ("brain", "slab")
    in_specs = (P(None, part, None, None), P(), P(), P(), P(), P(), P(part, None), P(part, None), P(part))
    body = functools.partial(local, mesh.shape["slab"])
    return jax.shard_map(body, mesh=mesh, in_specs=in_specs, out_specs=P(None, part, None, None), check_vma=False)
```

```python
import functools
import jax
import jax.numpy as jnp
from jax import lax
from jax.experimental import pallas as pl
from jax.experimental.pallas import tpu as pltpu
from jax.sharding import PartitionSpec as P

PATCHES = 2
PATCH_ROWS = 8
MARGIN = 2
RIM = 4
PATCH_X = 10
MOST_ACQ = 8
PRIOR = 0.1
EPS = 1e-05
F32 = jnp.float32
BF16 = jnp.bfloat16
MIB = 1 << 20


def vmem():
    return pl.BlockSpec(memory_space=pltpu.VMEM)


def smem():
    return pl.BlockSpec(memory_space=pltpu.SMEM)


def prep_kernel(feat, own, to_a, *to_b):
    channels, planes, rows, cols = feat.shape
    even = lax.rem(lax.axis_index("slab"), 2) == 0
    a_first = jnp.where(even, planes - RIM, 0)
    b_first = jnp.where(even, 0, planes - RIM)
    for x in range(planes):
        turned = jnp.swapaxes(feat[:, x].astype(F32), 0, 1).astype(BF16)
        for p in range(PATCHES):
            own[p, x] = turned[p * PATCH_ROWS : (p + 1) * PATCH_ROWS]
    for p in range(PATCHES):
        to_a[p] = own[p, pl.ds(a_first, RIM)]
        to_b[p][...] = own[p, pl.ds(b_first, RIM)]


def column_of(table, folds, width):
    diag = lax.broadcasted_iota(jnp.int32, (width, width), 0) == lax.broadcasted_iota(jnp.int32, (width, width), 1)
    parts = []
    for f in range(folds):
        row = jnp.broadcast_to(table[f : f + 1, :], (width, width))
        parts.append(jnp.sum(jnp.where(diag, row, 0.0), axis=1, keepdims=True))
    return jnp.concatenate(parts, 0)


def head_tables(head_w, head_b, folds, classes, channels):
    rows = classes * 2 * folds
    row = lax.broadcasted_iota(jnp.int32, (rows, classes), 0)
    cls = lax.broadcasted_iota(jnp.int32, (rows, classes), 1)
    brow = lax.broadcasted_iota(jnp.int32, (rows, classes), 0)
    lane = lax.broadcasted_iota(jnp.int32, (channels, folds * channels), 1)
    chan = lax.broadcasted_iota(jnp.int32, (channels, folds * channels), 0)
    table = jnp.zeros((rows, folds * channels), F32)
    bias = jnp.zeros((rows, 1), F32)
    for f in range(folds):
        pick = (row // (2 * folds) == cls) & (row % folds == f)
        part = jnp.dot(pick.astype(F32).astype(BF16), head_w[f], preferred_element_type=F32).astype(BF16)
        place = (lane == chan + f * channels).astype(F32).astype(BF16)
        table = table + jnp.dot(part, place, preferred_element_type=F32)
        bias = bias + jnp.sum(jnp.where(pick, jnp.broadcast_to(head_b[f : f + 1, :], (rows, classes)), 0.0), axis=1, keepdims=True)
    table = table.astype(BF16)
    return jnp.concatenate([table, table], 1), bias


def gauss(position, length):
    scaled = (position - (length - 1) / 2.0) / (length / 4.0)
    return jnp.exp(-0.5 * scaled * scaled)


def fill_taps(taps, plane, source):
    rows, channels, cols = source.shape
    lane = lax.broadcasted_iota(jnp.int32, (channels, cols), 1)
    for h in range(rows):
        value = source[h]
        wide = value.astype(F32)
        left = jnp.where(lane == 0, 0.0, pltpu.roll(wide, 1, 1)).astype(BF16)
        right = jnp.where(lane == cols - 1, 0.0, pltpu.roll(wide, cols - 1, 1)).astype(BF16)
        taps[plane, h + 1] = jnp.concatenate([left, value, right], 0)


def conv_planes(first, begin, end, fresh, taps, w_all, conv, stats):
    zero_plane = taps.shape[0] - 1
    cols = taps.shape[-1]

    def one_plane(x):
        i = first + x
        below = jnp.where(x == 0, zero_plane, i - 1)
        above = jnp.where(x == PATCH_X - 1, zero_plane, i + 1)
        weights = w_all[...]
        for r in range(PATCH_ROWS // 2):
            halves = []
            for h in (r, r + PATCH_ROWS // 2):
                halves.append(jnp.concatenate([taps[t, h : h + 3].reshape(-1, cols) for t in (below, i, above)], 0))
            out = jnp.dot(weights, jnp.concatenate(halves, 1), preferred_element_type=F32)
            conv[x, r] = out
            one, two = out[:, :cols], out[:, cols:]
            base = stats[0]
            if fresh and r == 0:
                base = jnp.where(x == begin, 0.5 * (one + two), base)
                stats[0] = base
            one, two = one - base, two - base
            stats[1] += one + two
            stats[2] += one * one + two * two

    def two_planes(y, _):
        one_plane(begin + 2 * y)
        one_plane(begin + 2 * y + 1)
        return 0

    def last_plane(y, _):
        one_plane(end - 1)
        return 0

    total = end - begin
    lax.fori_loop(0, total // 2, two_planes, 0)
    lax.fori_loop(0, lax.rem(total, 2), last_plane, 0)


def patch_plan(offs, p, planes):
    even = lax.rem(lax.axis_index("slab"), 2) == 0
    first = RIM - MARGIN + offs[0, p]
    foreign = jnp.where(even, RIM - first, first + PATCH_X - RIM - planes)
    foreign = foreign + jnp.minimum(foreign, 1)
    return even, first, jnp.where(even, foreign, 0), jnp.where(even, PATCH_X, PATCH_X - foreign)


def pre_kernel(offs, own, from_a, wt, gain, nbias, head_w, head_b, taps0, taps1, conv0, conv1, stats0, stats1, w_all, head, hbias, scales):
    planes = own.shape[1]
    folds, classes, channels = head_w.shape
    outs = folds * channels
    cols = own.shape[-1]
    span = planes + 2 * RIM
    even = lax.rem(lax.axis_index("slab"), 2) == 0
    a_base = jnp.where(even, RIM + planes, 0)
    wide_w = jnp.concatenate([wt[a].astype(F32) for a in range(3)], 0)
    w_all[...] = jnp.transpose(wide_w).astype(BF16)
    table, bias = head_tables(head_w, head_b, folds, classes, channels)
    head[...] = table
    hbias[...] = jnp.broadcast_to(bias, hbias.shape)
    scales[0] = jnp.broadcast_to(column_of(gain, folds, channels), (outs, cols))
    scales[1] = jnp.broadcast_to(column_of(nbias, folds, channels), (outs, cols))
    zero_row = jnp.zeros((3 * channels, cols), BF16)
    for p, (taps, conv, stats) in enumerate(((taps0, conv0, stats0), (taps1, conv1, stats1))):
        taps[span] = jnp.zeros(taps.shape[1:], BF16)

        def pad_rows(i, _):
            taps[i, 0] = zero_row
            taps[i, PATCH_ROWS + 1] = zero_row
            return 0

        def fill_own(i, _):
            fill_taps(taps, i + RIM, own.at[p, i])
            return 0

        def fill_a(i, _):
            fill_taps(taps, i + a_base, from_a.at[p, i])
            return 0

        lax.fori_loop(0, span, pad_rows, 0)
        lax.fori_loop(0, planes, fill_own, 0)
        lax.fori_loop(0, RIM, fill_a, 0)
        stats[...] = jnp.zeros_like(stats)
        _, first, begin, end = patch_plan(offs, p, planes)
        conv_planes(first, begin, end, True, taps, w_all, conv, stats)


def post_kernel(p, offs, mask, from_b, taps_in, conv_in, stats_in, w_all, head, hbias, scales, kept, to_a, to_b, taps, conv, stats, placed):
    planes = kept.shape[0] - 2
    span = taps.shape[0] - 1
    classes = kept.shape[1]
    outs, cols = stats.shape[1:]
    folds = head.shape[0] // classes // 2
    even, first, begin, end = patch_plan(offs, p, planes)
    b_base = jnp.where(even, 0, RIM + planes)

    def fill_b(i, _):
        fill_taps(taps, i + b_base, from_b.at[i])
        return 0

    lax.fori_loop(0, RIM, fill_b, 0)
    conv_planes(first, jnp.where(even, 0, end), jnp.where(even, begin, PATCH_X), False, taps, w_all, conv, stats)
    count = float(PATCH_X * PATCH_ROWS)
    total = stats[1] * (1.0 / count)
    spread = stats[2] - total * stats[1]
    lane_mean = stats[0] + total
    mean = jnp.mean(lane_mean, axis=1, keepdims=True)
    dev = lane_mean - mean
    var = jnp.sum(spread + count * dev * dev, axis=1, keepdims=True) * (1.0 / (count * cols))
    scale = lax.rsqrt(var + EPS) * scales[0, :, :1]
    scale_b = jnp.broadcast_to(scale, (outs, 2 * cols))
    offset_b = jnp.broadcast_to(scales[1, :, :1] - mean * scale, (outs, 2 * cols))
    keep = mask[0, p].astype(F32) * (1.0 / folds)
    placed[...] = jnp.zeros_like(placed)
    sub = lax.broadcasted_iota(jnp.int32, (2 * folds, cols), 0)
    lane = lax.broadcasted_iota(jnp.int32, (2 * folds, cols), 1)
    line = gauss(sub.astype(F32), PATCH_ROWS) * gauss(lane.astype(F32), cols)

    def finish_plane(x, _):
        lower = sub < folds
        table = [[] for _ in range(classes)]
        for r in range(PATCH_ROWS // 2):
            act = conv[x, r] * scale_b + offset_b
            act = jnp.maximum(act, 0.01 * act)
            high = act.astype(BF16)
            low = (act - high.astype(F32)).astype(BF16)
            logits = jnp.dot(head[...], jnp.concatenate([high, low], 0), preferred_element_type=F32) + hbias[...]
            parts = []
            for k in range(classes):
                both = logits[k * 2 * folds : (k + 1) * 2 * folds]
                parts.append(jnp.where(lower, both[:, :cols], both[:, cols:]))
            top = functools.reduce(jnp.maximum, parts)
            parts = [jnp.exp(v - top) for v in parts]
            denom = 1.0 / functools.reduce(jnp.add, parts)
            for k in range(classes):
                table[k].append(parts[k] * denom)
        window = line * (gauss(jnp.full((2 * folds, cols), x, jnp.int32).astype(F32), PATCH_X) * keep)
        odd = (sub % 2) == 1
        high_pair = (sub % 4) >= 2
        for k in range(classes):
            v = table[k]
            pairs = []
            for q in (0, 2):
                pairs.append(jnp.where(odd, v[q + 1] + pltpu.roll(v[q + 1], 1, 0), v[q] + pltpu.roll(v[q], 7, 0)))
            full = jnp.where(high_pair, pairs[1] + pltpu.roll(pairs[1], 2, 0), pairs[0] + pltpu.roll(pairs[0], 6, 0))
            placed[first + x, k] = full * window
        return 0

    lax.fori_loop(0, PATCH_X, finish_plane, 0)
    reach = RIM + 1
    kept[...] = placed[pl.ds(RIM - 1, planes + 2)]
    to_a[...] = placed[pl.ds(jnp.where(even, planes + RIM - 1, 0), reach)]
    to_b[...] = placed[pl.ds(jnp.where(even, 0, planes + RIM - 1), reach)]


def merge_kernel(slabs, acq, *refs):
    ins, out, merged = refs[:-2], refs[-2], refs[-1]
    wide = ins[0].shape[0]
    planes = wide - 2
    classes, rows, cols = ins[0].shape[1:]
    slab = lax.axis_index("slab")
    even = lax.rem(slab, 2) == 0
    a_base = jnp.where(even, wide - RIM - 1, 0)
    b_base = jnp.where(even, 0, wide - RIM - 1)
    shape = (rows, cols)
    count = jnp.full(shape, acq[0], jnp.int32).astype(F32)
    anchor = jnp.full(shape, slab * planes, jnp.int32).astype(F32)
    step = planes / jnp.maximum(count - 1.0, 1.0)
    for p in range(PATCHES):
        kept, from_a, from_b = ins[3 * p : 3 * p + 3]
        merged[...] = kept[...]
        merged[pl.ds(a_base, RIM + 1)] += from_a[...]
        merged[pl.ds(b_base, RIM + 1)] += from_b[...]
        table = []
        for j in range(wide):
            parts = [merged[j, k] for k in range(classes)]
            scale = 1.0 / (functools.reduce(jnp.add, parts) + PRIOR)
            parts[0] = parts[0] + PRIOR
            table.append([v * scale for v in parts])
        for s in range(MOST_ACQ):
            place = jnp.clip(anchor + (s * step - 0.5), 0.0, float(slabs * planes - 1)) - anchor
            used = (s < count).astype(F32)
            gains = [jnp.maximum(0.0, 1.0 - jnp.abs(place - (j - 1.0))) * used for j in range(wide)]
            for k in range(classes):
                out[k, s, p * rows : (p + 1) * rows] = functools.reduce(jnp.add, [gains[j] * table[j][k] for j in range(wide)])


def local(slabs, features, conv_weight, norm_gain, norm_bias, head_weight, head_bias, patch_offsets, fg_mask, acq_counts):
    channels, planes, row_total, cols = features.shape
    folds, classes, _ = head_weight.shape
    outs = folds * channels
    pairs_a = [(i, i ^ 1) for i in range(slabs) if (i ^ 1) < slabs]
    pairs_b = [(i, ((i + 1) ^ 1) - 1) for i in range(slabs) if 0 <= ((i + 1) ^ 1) - 1 < slabs]
    shaped = jax.ShapeDtypeStruct
    cell = (PATCH_ROWS, channels, cols)
    params = pltpu.CompilerParams(vmem_limit_bytes=24 * MIB)
    own, to_a, *to_b = pl.pallas_call(
        prep_kernel,
        out_shape=[shaped((PATCHES, planes) + cell, BF16), shaped((PATCHES, RIM) + cell, BF16)] + [shaped((RIM,) + cell, BF16)] * PATCHES,
        in_specs=[vmem()],
        out_specs=[vmem()] * (2 + PATCHES),
        compiler_params=params,
        name="prep",
    )(features)
    from_a = lax.ppermute(to_a, "slab", pairs_a)
    from_b = [lax.ppermute(v, "slab", pairs_b) for v in to_b]
    wide = planes + 2
    tile = (classes, PATCH_ROWS, cols)
    span = planes + 2 * RIM
    taps_shape = shaped((span + 1, PATCH_ROWS + 2, 3 * channels, cols), BF16)
    conv_shape = shaped((PATCH_X, PATCH_ROWS // 2, outs, 2 * cols), F32)
    stats_shape = shaped((3, outs, cols), F32)
    table_shapes = [shaped((outs, 27 * channels), BF16), shaped((classes * 2 * folds, 2 * outs), BF16), shaped((classes * 2 * folds, 2 * cols), F32), shaped((2, outs, cols), F32)]
    made = pl.pallas_call(
        pre_kernel,
        out_shape=[taps_shape] * 2 + [conv_shape] * 2 + [stats_shape] * 2 + table_shapes,
        in_specs=[smem()] + [vmem()] * 7,
        out_specs=[vmem()] * 10,
        compiler_params=params,
        name="pre",
    )(patch_offsets, own, from_a, jnp.swapaxes(conv_weight, 1, 2), norm_gain, norm_bias, head_weight, head_bias)
    merged_in = []
    for p in range(PATCHES):
        kept, send_a, send_b, *_ = pl.pallas_call(
            functools.partial(post_kernel, p),
            out_shape=[shaped((n,) + tile, F32) for n in (wide, RIM + 1, RIM + 1)] + [taps_shape, conv_shape, stats_shape],
            in_specs=[smem()] * 2 + [vmem()] * 8,
            out_specs=[vmem()] * 6,
            input_output_aliases={3: 3, 4: 4, 5: 5},
            scratch_shapes=[pltpu.VMEM((span,) + tile, F32)],
            compiler_params=params,
            name=f"post{p}",
        )(patch_offsets, fg_mask, from_b[p], made[p], made[2 + p], made[4 + p], *made[6:])
        merged_in += [kept, lax.ppermute(send_a, "slab", pairs_a), lax.ppermute(send_b, "slab", pairs_b)]
    return pl.pallas_call(
        functools.partial(merge_kernel, slabs),
        out_shape=shaped((classes, MOST_ACQ, row_total, cols), F32),
        in_specs=[smem()] + [vmem()] * (3 * PATCHES),
        out_specs=vmem(),
        scratch_shapes=[pltpu.VMEM((wide,) + tile, F32)],
        compiler_params=params,
        name="merge",
    )(acq_counts, *merged_in)


def solution(mesh):
    part = ("brain", "slab")
    in_specs = (P(None, part, None, None), P(), P(), P(), P(), P(), P(part, None), P(part, None), P(part))
    body = functools.partial(local, mesh.shape["slab"])
    return jax.shard_map(body, mesh=mesh, in_specs=in_specs, out_specs=P(None, part, None, None), check_vma=False)
```

```python
import functools
import jax
import jax.numpy as jnp
from jax import lax
from jax.experimental import pallas as pl
from jax.experimental.pallas import tpu as pltpu
from jax.sharding import PartitionSpec as P

PATCHES = 2
PATCH_ROWS = 8
MARGIN = 2
RIM = 4
PATCH_X = 10
MOST_ACQ = 8
PRIOR = 0.1
EPS = 1e-05
F32 = jnp.float32
BF16 = jnp.bfloat16
MIB = 1 << 20


def vmem():
    return pl.BlockSpec(memory_space=pltpu.VMEM)


def smem():
    return pl.BlockSpec(memory_space=pltpu.SMEM)


def prep_kernel(*refs):
    small = (len(refs) - 3 - 2 - PATCHES) // 2
    feat, small_in, rest = refs[0], refs[1 : 1 + small], refs[1 + small :]
    (own, to_a), to_b, small_out = rest[:2], rest[2 : 2 + PATCHES], rest[2 + PATCHES : 2 + PATCHES + small]
    held, sems = rest[2 + PATCHES + small :]
    channels, planes, rows, cols = feat.shape
    copies = [pltpu.make_async_copy(feat.at[:, x], held.at[x], sems.at[x]) for x in range(planes)]
    copies += [pltpu.make_async_copy(a, b, sems.at[planes + i]) for i, (a, b) in enumerate(zip(small_in, small_out))]
    for copy in copies:
        copy.start()
    even = lax.rem(lax.axis_index("slab"), 2) == 0
    a_first = jnp.where(even, planes - RIM, 0)
    b_first = jnp.where(even, 0, planes - RIM)
    for x in range(planes):
        copies[x].wait()
        turned = jnp.swapaxes(held[x].astype(F32), 0, 1).astype(BF16)
        for p in range(PATCHES):
            own[p, x] = turned[p * PATCH_ROWS : (p + 1) * PATCH_ROWS]
    for p in range(PATCHES):
        to_a[p] = own[p, pl.ds(a_first, RIM)]
        to_b[p][...] = own[p, pl.ds(b_first, RIM)]
    for copy in copies[planes:]:
        copy.wait()


def column_of(table, folds, width):
    diag = lax.broadcasted_iota(jnp.int32, (width, width), 0) == lax.broadcasted_iota(jnp.int32, (width, width), 1)
    parts = []
    for f in range(folds):
        row = jnp.broadcast_to(table[f : f + 1, :], (width, width))
        parts.append(jnp.sum(jnp.where(diag, row, 0.0), axis=1, keepdims=True))
    return jnp.concatenate(parts, 0)


def head_tables(head_w, head_b, folds, classes, channels):
    rows, outs = classes * 2 * folds, folds * channels
    lane = lax.broadcasted_iota(jnp.int32, (channels, outs), 1)
    chan = lax.broadcasted_iota(jnp.int32, (channels, outs), 0)
    spread = (lane % channels == chan).astype(F32).astype(BF16)
    tall = []
    for k in range(classes):
        tall += [head_w[k].astype(F32)] * 2
    tall = jnp.concatenate(tall, 0).astype(BF16)
    table = jnp.dot(tall, spread, preferred_element_type=F32)
    row = lax.broadcasted_iota(jnp.int32, (rows, outs), 0)
    col = lax.broadcasted_iota(jnp.int32, (rows, outs), 1)
    table = jnp.where(row % folds == col // channels, table, 0.0).astype(BF16)
    row = lax.broadcasted_iota(jnp.int32, (rows, classes), 0)
    cls = lax.broadcasted_iota(jnp.int32, (rows, classes), 1)
    bias = jnp.zeros((rows, 1), F32)
    for f in range(folds):
        pick = (row // (2 * folds) == cls) & (row % folds == f)
        bias = bias + jnp.sum(jnp.where(pick, jnp.broadcast_to(head_b[f : f + 1, :], (rows, classes)), 0.0), axis=1, keepdims=True)
    return jnp.concatenate([table, table], 1), bias


def gauss(position, length):
    scaled = (position - (length - 1) / 2.0) / (length / 4.0)
    return jnp.exp(-0.5 * scaled * scaled)


def fill_taps(taps, plane, source):
    rows, channels, cols = source.shape
    lane = lax.broadcasted_iota(jnp.int32, (channels, cols), 1)
    for h in range(rows):
        value = source[h]
        wide = value.astype(F32)
        left = jnp.where(lane == 0, 0.0, pltpu.roll(wide, 1, 1)).astype(BF16)
        right = jnp.where(lane == cols - 1, 0.0, pltpu.roll(wide, cols - 1, 1)).astype(BF16)
        taps[plane, h + 1] = jnp.concatenate([left, value, right], 0)


def conv_planes(first, begin, end, fresh, taps, w_all, conv, stats):
    zero_plane = taps.shape[0] - 1
    cols = taps.shape[-1]

    def one_plane(x):
        i = first + x
        below = jnp.where(x == 0, zero_plane, i - 1)
        above = jnp.where(x == PATCH_X - 1, zero_plane, i + 1)
        weights = w_all[...]
        for r in range(PATCH_ROWS // 2):
            halves = []
            for h in (r, r + PATCH_ROWS // 2):
                halves.append(jnp.concatenate([taps[t, h : h + 3].reshape(-1, cols) for t in (below, i, above)], 0))
            out = jnp.dot(weights, jnp.concatenate(halves, 1), preferred_element_type=F32)
            conv[x, r] = out
            one, two = out[:, :cols], out[:, cols:]
            base = stats[0]
            if fresh and r == 0:
                base = jnp.where(x == begin, 0.5 * (one + two), base)
                stats[0] = base
            one, two = one - base, two - base
            stats[1] += one + two
            stats[2] += one * one + two * two

    def two_planes(y, _):
        one_plane(begin + 2 * y)
        one_plane(begin + 2 * y + 1)
        return 0

    def last_plane(y, _):
        one_plane(end - 1)
        return 0

    total = end - begin
    lax.fori_loop(0, total // 2, two_planes, 0)
    lax.fori_loop(0, lax.rem(total, 2), last_plane, 0)


def patch_plan(offs, p, planes):
    even = lax.rem(lax.axis_index("slab"), 2) == 0
    first = RIM - MARGIN + offs[0, p]
    foreign = jnp.where(even, RIM - first, first + PATCH_X - RIM - planes)
    foreign = foreign + jnp.minimum(foreign, 1)
    return even, first, jnp.where(even, foreign, 0), jnp.where(even, PATCH_X, PATCH_X - foreign)


def pre_kernel(offs, own, from_a, wt, gain, nbias, head_w, head_b, taps0, taps1, conv0, conv1, stats0, stats1, w_all, head, hbias, scales):
    planes = own.shape[1]
    classes, folds, channels = head_w.shape
    outs = folds * channels
    cols = own.shape[-1]
    span = planes + 2 * RIM
    even = lax.rem(lax.axis_index("slab"), 2) == 0
    a_base = jnp.where(even, RIM + planes, 0)
    eye = (lax.broadcasted_iota(jnp.int32, (outs, outs), 0) == lax.broadcasted_iota(jnp.int32, (outs, outs), 1)).astype(F32).astype(BF16)
    wide_w = jnp.concatenate([wt[a] for a in range(3)], 0)
    w_all[...] = lax.dot_general(eye, wide_w, (((1,), (1,)), ((), ())), preferred_element_type=F32).astype(BF16)
    table, bias = head_tables(head_w, head_b, folds, classes, channels)
    head[...] = table
    hbias[...] = jnp.broadcast_to(bias, hbias.shape)
    scales[0] = jnp.broadcast_to(column_of(gain, folds, channels), (outs, cols))
    scales[1] = jnp.broadcast_to(column_of(nbias, folds, channels), (outs, cols))
    zero_row = jnp.zeros((3 * channels, cols), BF16)
    for p, (taps, conv, stats) in enumerate(((taps0, conv0, stats0), (taps1, conv1, stats1))):
        taps[span] = jnp.zeros(taps.shape[1:], BF16)

        def pad_rows(i, _):
            taps[i, 0] = zero_row
            taps[i, PATCH_ROWS + 1] = zero_row
            return 0

        def fill_own(i, _):
            fill_taps(taps, i + RIM, own.at[p, i])
            return 0

        def fill_a(i, _):
            fill_taps(taps, i + a_base, from_a.at[p, i])
            return 0

        lax.fori_loop(0, span, pad_rows, 0)
        lax.fori_loop(0, planes, fill_own, 0, unroll=2)
        lax.fori_loop(0, RIM, fill_a, 0, unroll=2)
        stats[...] = jnp.zeros_like(stats)
        _, first, begin, end = patch_plan(offs, p, planes)
        conv_planes(first, begin, end, True, taps, w_all, conv, stats)


def post_kernel(p, offs, mask, from_b, taps_in, conv_in, stats_in, w_all, head, hbias, scales, *refs):
    kept, to_a, to_b, taps, conv, stats, placed = refs[-7:]
    planes = kept.shape[1] - 2
    classes = kept.shape[2]
    outs, cols = stats.shape[1:]
    folds = head.shape[0] // classes // 2
    even, first, begin, end = patch_plan(offs, p, planes)
    b_base = jnp.where(even, 0, RIM + planes)

    def fill_b(i, _):
        fill_taps(taps, i + b_base, from_b.at[i])
        return 0

    lax.fori_loop(0, RIM, fill_b, 0, unroll=2)
    conv_planes(first, jnp.where(even, 0, end), jnp.where(even, begin, PATCH_X), False, taps, w_all, conv, stats)
    count = float(PATCH_X * PATCH_ROWS)
    total = stats[1] * (1.0 / count)
    spread = stats[2] - total * stats[1]
    lane_mean = stats[0] + total
    mean = jnp.mean(lane_mean, axis=1, keepdims=True)
    dev = lane_mean - mean
    var = jnp.sum(spread + count * dev * dev, axis=1, keepdims=True) * (1.0 / (count * cols))
    scale = lax.rsqrt(var + EPS) * scales[0, :, :1]
    scale_b = jnp.broadcast_to(scale, (outs, 2 * cols))
    offset_b = jnp.broadcast_to(scales[1, :, :1] - mean * scale, (outs, 2 * cols))
    keep = mask[0, p].astype(F32) * (1.0 / folds)
    placed[...] = jnp.zeros_like(placed)
    sub = lax.broadcasted_iota(jnp.int32, (2 * folds, cols), 0)
    lane = lax.broadcasted_iota(jnp.int32, (2 * folds, cols), 1)
    line = gauss(sub.astype(F32), PATCH_ROWS) * gauss(lane.astype(F32), cols)

    def finish_plane(x, _):
        lower = sub < folds
        table = [[] for _ in range(classes)]
        for r in range(PATCH_ROWS // 2):
            act = conv[x, r] * scale_b + offset_b
            act = jnp.maximum(act, 0.01 * act)
            high = act.astype(BF16)
            low = (act - high.astype(F32)).astype(BF16)
            logits = jnp.dot(head[...], jnp.concatenate([high, low], 0), preferred_element_type=F32) + hbias[...]
            parts = []
            for k in range(classes):
                both = logits[k * 2 * folds : (k + 1) * 2 * folds]
                parts.append(jnp.where(lower, both[:, :cols], both[:, cols:]))
            top = functools.reduce(jnp.maximum, parts)
            parts = [jnp.exp(v - top) for v in parts]
            denom = 1.0 / functools.reduce(jnp.add, parts)
            for k in range(classes):
                table[k].append(parts[k] * denom)
        window = line * (gauss(jnp.full((2 * folds, cols), x, jnp.int32).astype(F32), PATCH_X) * keep)
        odd = (sub % 2) == 1
        high_pair = (sub % 4) >= 2
        for k in range(classes):
            v = table[k]
            pairs = []
            for q in (0, 2):
                pairs.append(jnp.where(odd, v[q + 1] + pltpu.roll(v[q + 1], 1, 0), v[q] + pltpu.roll(v[q], 7, 0)))
            full = jnp.where(high_pair, pairs[1] + pltpu.roll(pairs[1], 2, 0), pairs[0] + pltpu.roll(pairs[0], 6, 0))
            placed[first + x, k] = full * window
        return 0

    lax.fori_loop(0, PATCH_X, finish_plane, 0, unroll=2)
    reach = RIM + 1
    kept[p] = placed[pl.ds(RIM - 1, planes + 2)]
    to_a[p] = placed[pl.ds(jnp.where(even, planes + RIM - 1, 0), reach)]
    to_b[p] = placed[pl.ds(jnp.where(even, 0, planes + RIM - 1), reach)]


def merge_kernel(slabs, acq, kept, from_a, from_b, out, merged):
    wide = kept.shape[1]
    planes = wide - 2
    classes, rows, cols = kept.shape[2:]
    slab = lax.axis_index("slab")
    even = lax.rem(slab, 2) == 0
    a_base = jnp.where(even, wide - RIM - 1, 0)
    b_base = jnp.where(even, 0, wide - RIM - 1)
    shape = (rows, cols)
    count = jnp.full(shape, acq[0], jnp.int32).astype(F32)
    anchor = jnp.full(shape, slab * planes, jnp.int32).astype(F32)
    step = planes / jnp.maximum(count - 1.0, 1.0)
    for p in range(PATCHES):
        merged[...] = kept[p]
        merged[pl.ds(a_base, RIM + 1)] += from_a[p]
        merged[pl.ds(b_base, RIM + 1)] += from_b[p]
        table = []
        for j in range(wide):
            parts = [merged[j, k] for k in range(classes)]
            scale = 1.0 / (functools.reduce(jnp.add, parts) + PRIOR)
            parts[0] = parts[0] + PRIOR
            table.append([v * scale for v in parts])
        for s in range(MOST_ACQ):
            place = jnp.clip(anchor + (s * step - 0.5), 0.0, float(slabs * planes - 1)) - anchor
            used = (s < count).astype(F32)
            gains = [jnp.maximum(0.0, 1.0 - jnp.abs(place - (j - 1.0))) * used for j in range(wide)]
            for k in range(classes):
                out[k, s, p * rows : (p + 1) * rows] = functools.reduce(jnp.add, [gains[j] * table[j][k] for j in range(wide)])


def local(slabs, features, conv_weight, norm_gain, norm_bias, head_weight, head_bias, patch_offsets, fg_mask, acq_counts):
    channels, planes, row_total, cols = features.shape
    folds, classes, _ = head_weight.shape
    outs = folds * channels
    pairs_a = [(i, i ^ 1) for i in range(slabs) if (i ^ 1) < slabs]
    pairs_b = [(i, ((i + 1) ^ 1) - 1) for i in range(slabs) if 0 <= ((i + 1) ^ 1) - 1 < slabs]
    shaped = jax.ShapeDtypeStruct
    cell = (PATCH_ROWS, channels, cols)
    params = pltpu.CompilerParams(vmem_limit_bytes=24 * MIB)
    small = [jnp.swapaxes(conv_weight, 1, 2), norm_gain, norm_bias, jnp.swapaxes(head_weight, 0, 1), head_bias, patch_offsets, fg_mask]
    own, to_a, *rest = pl.pallas_call(
        prep_kernel,
        out_shape=[shaped((PATCHES, planes) + cell, BF16), shaped((PATCHES, RIM) + cell, BF16)]
        + [shaped((RIM,) + cell, BF16)] * PATCHES
        + [shaped(v.shape, v.dtype) for v in small],
        in_specs=[pl.BlockSpec(memory_space=pltpu.HBM)] * (1 + len(small)),
        out_specs=[vmem()] * (2 + PATCHES + len(small)),
        scratch_shapes=[pltpu.VMEM((planes, channels, row_total, cols), BF16), pltpu.SemaphoreType.DMA((planes + len(small),))],
        compiler_params=params,
        name="prep",
    )(*[pltpu.with_memory_space_constraint(v, pltpu.HBM) for v in (features, *small)])
    to_b, (conv_weight, norm_gain, norm_bias, head_weight, head_bias, patch_offsets, fg_mask) = rest[:PATCHES], rest[PATCHES:]
    from_a = lax.ppermute(to_a, "slab", pairs_a)
    from_b = [lax.ppermute(v, "slab", pairs_b) for v in to_b]
    wide = planes + 2
    tile = (classes, PATCH_ROWS, cols)
    span = planes + 2 * RIM
    taps_shape = shaped((span + 1, PATCH_ROWS + 2, 3 * channels, cols), BF16)
    conv_shape = shaped((PATCH_X, PATCH_ROWS // 2, outs, 2 * cols), F32)
    stats_shape = shaped((3, outs, cols), F32)
    table_shapes = [shaped((outs, 27 * channels), BF16), shaped((classes * 2 * folds, 2 * outs), BF16), shaped((classes * 2 * folds, 2 * cols), F32), shaped((2, outs, cols), F32)]
    made = pl.pallas_call(
        pre_kernel,
        out_shape=[taps_shape] * 2 + [conv_shape] * 2 + [stats_shape] * 2 + table_shapes,
        in_specs=[smem()] + [vmem()] * 7,
        out_specs=[vmem()] * 10,
        compiler_params=params,
        name="pre",
    )(patch_offsets, own, from_a, conv_weight, norm_gain, norm_bias, head_weight, head_bias)
    sends = []
    send_shapes = [shaped((PATCHES, n) + tile, F32) for n in (wide, RIM + 1, RIM + 1)]
    for p in range(PATCHES):
        sends = pl.pallas_call(
            functools.partial(post_kernel, p),
            out_shape=send_shapes + [taps_shape, conv_shape, stats_shape],
            in_specs=[smem()] * 2 + [vmem()] * (8 + len(sends)),
            out_specs=[vmem()] * 6,
            input_output_aliases={3: 3, 4: 4, 5: 5} | {10 + i: i for i in range(len(sends))},
            scratch_shapes=[pltpu.VMEM((span,) + tile, F32)],
            compiler_params=params,
            name=f"post{p}",
        )(patch_offsets, fg_mask, from_b[p], made[p], made[2 + p], made[4 + p], *made[6:], *sends)[:3]
    kept, send_a, send_b = sends
    return pl.pallas_call(
        functools.partial(merge_kernel, slabs),
        out_shape=shaped((classes, MOST_ACQ, row_total, cols), F32),
        in_specs=[smem()] + [vmem()] * 3,
        out_specs=vmem(),
        scratch_shapes=[pltpu.VMEM((wide,) + tile, F32)],
        compiler_params=params,
        name="merge",
    )(acq_counts, kept, lax.ppermute(send_a, "slab", pairs_a), lax.ppermute(send_b, "slab", pairs_b))


def solution(mesh):
    part = ("brain", "slab")
    in_specs = (P(None, part, None, None), P(), P(), P(), P(), P(), P(part, None), P(part, None), P(part))
    body = functools.partial(local, mesh.shape["slab"])
    return jax.shard_map(body, mesh=mesh, in_specs=in_specs, out_specs=P(None, part, None, None), check_vma=False)
```

```python
import functools
import jax
import jax.numpy as jnp
from jax import lax
from jax.experimental import pallas as pl
from jax.experimental.pallas import tpu as pltpu
from jax.sharding import PartitionSpec as P

PATCHES = 2
PATCH_ROWS = 8
MARGIN = 2
RIM = 4
PATCH_X = 10
MOST_ACQ = 8
PRIOR = 0.1
EPS = 1e-05
F32 = jnp.float32
BF16 = jnp.bfloat16
MIB = 1 << 20
UNIT = 32767.0


def vmem():
    return pl.BlockSpec(memory_space=pltpu.VMEM)


def smem():
    return pl.BlockSpec(memory_space=pltpu.SMEM)


def prep_kernel(*refs):
    small = (len(refs) - 3 - 2 - PATCHES) // 2
    feat, small_in, rest = refs[0], refs[1 : 1 + small], refs[1 + small :]
    (own, to_a), to_b, small_out = rest[:2], rest[2 : 2 + PATCHES], rest[2 + PATCHES : 2 + PATCHES + small]
    held, sems = rest[2 + PATCHES + small :]
    channels, planes, rows, cols = feat.shape
    copies = [pltpu.make_async_copy(feat.at[:, x], held.at[x], sems.at[x]) for x in range(planes)]
    copies += [pltpu.make_async_copy(a, b, sems.at[planes + i]) for i, (a, b) in enumerate(zip(small_in, small_out))]
    for copy in copies:
        copy.start()
    even = lax.rem(lax.axis_index("slab"), 2) == 0
    a_first = jnp.where(even, planes - RIM, 0)
    b_first = jnp.where(even, 0, planes - RIM)
    for x in range(planes):
        copies[x].wait()
        turned = jnp.swapaxes(held[x].astype(F32), 0, 1).astype(BF16)
        for p in range(PATCHES):
            own[p, x] = turned[p * PATCH_ROWS : (p + 1) * PATCH_ROWS]
    for p in range(PATCHES):
        to_a[p] = own[p, pl.ds(a_first, RIM)]
        to_b[p][...] = own[p, pl.ds(b_first, RIM)]
    for copy in copies[planes:]:
        copy.wait()


def column_of(table, folds, width):
    diag = lax.broadcasted_iota(jnp.int32, (width, width), 0) == lax.broadcasted_iota(jnp.int32, (width, width), 1)
    parts = []
    for f in range(folds):
        row = jnp.broadcast_to(table[f : f + 1, :], (width, width))
        parts.append(jnp.sum(jnp.where(diag, row, 0.0), axis=1, keepdims=True))
    return jnp.concatenate(parts, 0)


def head_tables(head_w, head_b, folds, classes, channels):
    rows, outs = classes * 2 * folds, folds * channels
    lane = lax.broadcasted_iota(jnp.int32, (channels, outs), 1)
    chan = lax.broadcasted_iota(jnp.int32, (channels, outs), 0)
    spread = (lane % channels == chan).astype(F32).astype(BF16)
    tall = []
    for k in range(classes):
        tall += [head_w[k].astype(F32)] * 2
    tall = jnp.concatenate(tall, 0).astype(BF16)
    table = jnp.dot(tall, spread, preferred_element_type=F32)
    row = lax.broadcasted_iota(jnp.int32, (rows, outs), 0)
    col = lax.broadcasted_iota(jnp.int32, (rows, outs), 1)
    table = jnp.where(row % folds == col // channels, table, 0.0).astype(BF16)
    row = lax.broadcasted_iota(jnp.int32, (rows, classes), 0)
    cls = lax.broadcasted_iota(jnp.int32, (rows, classes), 1)
    bias = jnp.zeros((rows, 1), F32)
    for f in range(folds):
        pick = (row // (2 * folds) == cls) & (row % folds == f)
        bias = bias + jnp.sum(jnp.where(pick, jnp.broadcast_to(head_b[f : f + 1, :], (rows, classes)), 0.0), axis=1, keepdims=True)
    return jnp.concatenate([table, table], 1), bias


def gauss(position, length):
    scaled = (position - (length - 1) / 2.0) / (length / 4.0)
    return jnp.exp(-0.5 * scaled * scaled)


def fill_taps(taps, plane, source):
    rows, channels, cols = source.shape
    lane = lax.broadcasted_iota(jnp.int32, (channels, cols), 1)
    for h in range(rows):
        value = source[h]
        wide = value.astype(F32)
        left = jnp.where(lane == 0, 0.0, pltpu.roll(wide, 1, 1)).astype(BF16)
        right = jnp.where(lane == cols - 1, 0.0, pltpu.roll(wide, cols - 1, 1)).astype(BF16)
        taps[plane, h + 1] = jnp.concatenate([left, value, right], 0)


def conv_planes(first, begin, end, fresh, taps, w_all, conv, stats):
    zero_plane = taps.shape[0] - 1
    cols = taps.shape[-1]

    def one_plane(x):
        i = first + x
        below = jnp.where(x == 0, zero_plane, i - 1)
        above = jnp.where(x == PATCH_X - 1, zero_plane, i + 1)
        weights = w_all[...]
        for r in range(PATCH_ROWS // 2):
            halves = []
            for h in (r, r + PATCH_ROWS // 2):
                halves.append(jnp.concatenate([taps[t, h : h + 3].reshape(-1, cols) for t in (below, i, above)], 0))
            out = jnp.dot(weights, jnp.concatenate(halves, 1), preferred_element_type=F32)
            conv[x, r] = out
            one, two = out[:, :cols], out[:, cols:]
            base = stats[0]
            if fresh and r == 0:
                base = jnp.where(x == begin, 0.5 * (one + two), base)
                stats[0] = base
            one, two = one - base, two - base
            stats[1] += one + two
            stats[2] += one * one + two * two

    def two_planes(y, _):
        one_plane(begin + 2 * y)
        one_plane(begin + 2 * y + 1)
        return 0

    def last_plane(y, _):
        one_plane(end - 1)
        return 0

    total = end - begin
    lax.fori_loop(0, total // 2, two_planes, 0)
    lax.fori_loop(0, lax.rem(total, 2), last_plane, 0)


def patch_plan(offs, p, planes):
    even = lax.rem(lax.axis_index("slab"), 2) == 0
    first = RIM - MARGIN + offs[0, p]
    foreign = jnp.where(even, RIM - first, first + PATCH_X - RIM - planes)
    foreign = foreign + jnp.minimum(foreign, 1)
    return even, first, jnp.where(even, foreign, 0), jnp.where(even, PATCH_X, PATCH_X - foreign)


def pre_kernel(offs, own, from_a, wt, gain, nbias, head_w, head_b, taps0, taps1, conv0, conv1, stats0, stats1, w_all, head, hbias, scales):
    planes = own.shape[1]
    classes, folds, channels = head_w.shape
    outs = folds * channels
    cols = own.shape[-1]
    span = planes + 2 * RIM
    even = lax.rem(lax.axis_index("slab"), 2) == 0
    a_base = jnp.where(even, RIM + planes, 0)
    eye = (lax.broadcasted_iota(jnp.int32, (outs, outs), 0) == lax.broadcasted_iota(jnp.int32, (outs, outs), 1)).astype(F32).astype(BF16)
    wide_w = jnp.concatenate([wt[a] for a in range(3)], 0)
    w_all[...] = lax.dot_general(eye, wide_w, (((1,), (1,)), ((), ())), preferred_element_type=F32).astype(BF16)
    table, bias = head_tables(head_w, head_b, folds, classes, channels)
    head[...] = table
    hbias[...] = jnp.broadcast_to(bias, hbias.shape)
    scales[0] = jnp.broadcast_to(column_of(gain, folds, channels), (outs, cols))
    scales[1] = jnp.broadcast_to(column_of(nbias, folds, channels), (outs, cols))
    zero_row = jnp.zeros((3 * channels, cols), BF16)
    for p, (taps, conv, stats) in enumerate(((taps0, conv0, stats0), (taps1, conv1, stats1))):
        taps[span] = jnp.zeros(taps.shape[1:], BF16)

        def pad_rows(i, _):
            taps[i, 0] = zero_row
            taps[i, PATCH_ROWS + 1] = zero_row
            return 0

        def fill_own(i, _):
            fill_taps(taps, i + RIM, own.at[p, i])
            return 0

        def fill_a(i, _):
            fill_taps(taps, i + a_base, from_a.at[p, i])
            return 0

        lax.fori_loop(0, span, pad_rows, 0)
        lax.fori_loop(0, planes, fill_own, 0, unroll=2)
        lax.fori_loop(0, RIM, fill_a, 0, unroll=2)
        stats[...] = jnp.zeros_like(stats)
        _, first, begin, end = patch_plan(offs, p, planes)
        conv_planes(first, begin, end, True, taps, w_all, conv, stats)


def post_kernel(p, offs, mask, from_b, taps_in, conv_in, stats_in, w_all, head, hbias, scales, *refs):
    kept, to_a, to_b, taps, conv, stats, placed = refs[-7:]
    planes = kept.shape[1] - 2
    classes = kept.shape[2]
    outs, cols = stats.shape[1:]
    folds = head.shape[0] // classes // 2
    even, first, begin, end = patch_plan(offs, p, planes)
    b_base = jnp.where(even, 0, RIM + planes)

    def fill_b(i, _):
        fill_taps(taps, i + b_base, from_b.at[i])
        return 0

    lax.fori_loop(0, RIM, fill_b, 0, unroll=2)
    conv_planes(first, jnp.where(even, 0, end), jnp.where(even, begin, PATCH_X), False, taps, w_all, conv, stats)
    count = float(PATCH_X * PATCH_ROWS)
    total = stats[1] * (1.0 / count)
    spread = stats[2] - total * stats[1]
    lane_mean = stats[0] + total
    mean = jnp.mean(lane_mean, axis=1, keepdims=True)
    dev = lane_mean - mean
    var = jnp.sum(spread + count * dev * dev, axis=1, keepdims=True) * (1.0 / (count * cols))
    scale = lax.rsqrt(var + EPS) * scales[0, :, :1]
    scale_b = jnp.broadcast_to(scale, (outs, 2 * cols))
    offset_b = jnp.broadcast_to(scales[1, :, :1] - mean * scale, (outs, 2 * cols))
    keep = mask[0, p].astype(F32) * (1.0 / folds)
    placed[...] = jnp.zeros_like(placed)
    sub = lax.broadcasted_iota(jnp.int32, (2 * folds, cols), 0)
    lane = lax.broadcasted_iota(jnp.int32, (2 * folds, cols), 1)
    line = gauss(sub.astype(F32), PATCH_ROWS) * gauss(lane.astype(F32), cols)

    def finish_plane(x, _):
        lower = sub < folds
        table = [[] for _ in range(classes)]
        for r in range(PATCH_ROWS // 2):
            act = conv[x, r] * scale_b + offset_b
            act = jnp.maximum(act, 0.01 * act)
            high = act.astype(BF16)
            low = (act - high.astype(F32)).astype(BF16)
            logits = jnp.dot(head[...], jnp.concatenate([high, low], 0), preferred_element_type=F32) + hbias[...]
            parts = []
            for k in range(classes):
                both = logits[k * 2 * folds : (k + 1) * 2 * folds]
                parts.append(jnp.where(lower, both[:, :cols], both[:, cols:]))
            top = functools.reduce(jnp.maximum, parts)
            parts = [jnp.exp(v - top) for v in parts]
            denom = 1.0 / functools.reduce(jnp.add, parts)
            for k in range(classes):
                table[k].append(parts[k] * denom)
        window = line * (gauss(jnp.full((2 * folds, cols), x, jnp.int32).astype(F32), PATCH_X) * keep)
        odd = (sub % 2) == 1
        high_pair = (sub % 4) >= 2
        for k in range(classes):
            v = table[k]
            pairs = []
            for q in (0, 2):
                pairs.append(jnp.where(odd, v[q + 1] + pltpu.roll(v[q + 1], 1, 0), v[q] + pltpu.roll(v[q], 7, 0)))
            full = jnp.where(high_pair, pairs[1] + pltpu.roll(pairs[1], 2, 0), pairs[0] + pltpu.roll(pairs[0], 6, 0))
            placed[first + x, k] = full * window
        return 0

    lax.fori_loop(0, PATCH_X, finish_plane, 0, unroll=2)
    reach = RIM + 1
    kept[p] = placed[pl.ds(RIM - 1, planes + 2)]
    for send, begin in ((to_a, jnp.where(even, planes + RIM - 1, 0)), (to_b, jnp.where(even, 0, planes + RIM - 1))):
        for j in range(reach):
            send[p, j] = (placed[begin + j] * UNIT + 0.5).astype(jnp.int32).astype(jnp.int16)


def merge_kernel(slabs, acq, kept, from_a, from_b, out, merged, held, sems):
    wide = kept.shape[1]
    planes = wide - 2
    classes, rows, cols = kept.shape[2:]
    slab = lax.axis_index("slab")
    even = lax.rem(slab, 2) == 0
    a_base = jnp.where(even, wide - RIM - 1, 0)
    b_base = jnp.where(even, 0, wide - RIM - 1)
    shape = (rows, cols)
    count = jnp.full(shape, acq[0], jnp.int32).astype(F32)
    anchor = jnp.full(shape, slab * planes, jnp.int32).astype(F32)
    step = planes / jnp.maximum(count - 1.0, 1.0)
    for p in range(PATCHES):
        merged[p] = kept[p]
        for base, got in ((a_base, from_a), (b_base, from_b)):
            for j in range(RIM + 1):
                merged[p, base + j] += got[p, j].astype(jnp.int32).astype(F32) * (1.0 / UNIT)
        for j in range(wide):
            parts = [merged[p, j, k] for k in range(classes)]
            scale = 1.0 / (functools.reduce(jnp.add, parts) + PRIOR)
            parts[0] = parts[0] + PRIOR
            for k in range(classes):
                merged[p, j, k] = parts[k] * scale
    gains = []
    for s in range(MOST_ACQ):
        place = jnp.clip(anchor + (s * step - 0.5), 0.0, float(slabs * planes - 1)) - anchor
        used = (s < count).astype(F32)
        gains.append([jnp.maximum(0.0, 1.0 - jnp.abs(place - (j - 1.0))) * used for j in range(wide)])
    copies = []
    for k in range(classes):
        for p in range(PATCHES):
            column = [merged[p, j, k] for j in range(wide)]
            for s in range(MOST_ACQ):
                held[k, s, p * rows : (p + 1) * rows] = functools.reduce(jnp.add, [g * v for g, v in zip(gains[s], column)])
        copies.append(pltpu.make_async_copy(held.at[k], out.at[k], sems.at[k]))
        copies[-1].start()
    for copy in copies:
        copy.wait()


def local(slabs, features, conv_weight, norm_gain, norm_bias, head_weight, head_bias, patch_offsets, fg_mask, acq_counts):
    channels, planes, row_total, cols = features.shape
    folds, classes, _ = head_weight.shape
    outs = folds * channels
    pairs_a = [(i, i ^ 1) for i in range(slabs) if (i ^ 1) < slabs]
    pairs_b = [(i, ((i + 1) ^ 1) - 1) for i in range(slabs) if 0 <= ((i + 1) ^ 1) - 1 < slabs]
    shaped = jax.ShapeDtypeStruct
    cell = (PATCH_ROWS, channels, cols)
    params = pltpu.CompilerParams(vmem_limit_bytes=24 * MIB)
    small = [jnp.swapaxes(conv_weight, 1, 2), norm_gain, norm_bias, jnp.swapaxes(head_weight, 0, 1), head_bias, patch_offsets, fg_mask]
    own, to_a, *rest = pl.pallas_call(
        prep_kernel,
        out_shape=[shaped((PATCHES, planes) + cell, BF16), shaped((PATCHES, RIM) + cell, BF16)]
        + [shaped((RIM,) + cell, BF16)] * PATCHES
        + [shaped(v.shape, v.dtype) for v in small],
        in_specs=[pl.BlockSpec(memory_space=pltpu.HBM)] * (1 + len(small)),
        out_specs=[vmem()] * (2 + PATCHES + len(small)),
        scratch_shapes=[pltpu.VMEM((planes, channels, row_total, cols), BF16), pltpu.SemaphoreType.DMA((planes + len(small),))],
        compiler_params=params,
        name="prep",
    )(*[pltpu.with_memory_space_constraint(v, pltpu.HBM) for v in (features, *small)])
    to_b, (conv_weight, norm_gain, norm_bias, head_weight, head_bias, patch_offsets, fg_mask) = rest[:PATCHES], rest[PATCHES:]
    from_a = lax.ppermute(to_a, "slab", pairs_a)
    from_b = [lax.ppermute(v, "slab", pairs_b) for v in to_b]
    wide = planes + 2
    tile = (classes, PATCH_ROWS, cols)
    span = planes + 2 * RIM
    taps_shape = shaped((span + 1, PATCH_ROWS + 2, 3 * channels, cols), BF16)
    conv_shape = shaped((PATCH_X, PATCH_ROWS // 2, outs, 2 * cols), F32)
    stats_shape = shaped((3, outs, cols), F32)
    table_shapes = [shaped((outs, 27 * channels), BF16), shaped((classes * 2 * folds, 2 * outs), BF16), shaped((classes * 2 * folds, 2 * cols), F32), shaped((2, outs, cols), F32)]
    made = pl.pallas_call(
        pre_kernel,
        out_shape=[taps_shape] * 2 + [conv_shape] * 2 + [stats_shape] * 2 + table_shapes,
        in_specs=[smem()] + [vmem()] * 7,
        out_specs=[vmem()] * 10,
        compiler_params=params,
        name="pre",
    )(patch_offsets, own, from_a, conv_weight, norm_gain, norm_bias, head_weight, head_bias)
    sends = []
    send_shapes = [shaped((PATCHES, n) + tile, t) for n, t in ((wide, F32), (RIM + 1, jnp.int16), (RIM + 1, jnp.int16))]
    for p in range(PATCHES):
        sends = pl.pallas_call(
            functools.partial(post_kernel, p),
            out_shape=send_shapes + [taps_shape, conv_shape, stats_shape],
            in_specs=[smem()] * 2 + [vmem()] * (8 + len(sends)),
            out_specs=[vmem()] * 6,
            input_output_aliases={3: 3, 4: 4, 5: 5} | {10 + i: i for i in range(len(sends))},
            scratch_shapes=[pltpu.VMEM((span,) + tile, F32)],
            compiler_params=params,
            name=f"post{p}",
        )(patch_offsets, fg_mask, from_b[p], made[p], made[2 + p], made[4 + p], *made[6:], *sends)[:3]
    kept, send_a, send_b = sends
    return pl.pallas_call(
        functools.partial(merge_kernel, slabs),
        out_shape=shaped((classes, MOST_ACQ, row_total, cols), F32),
        in_specs=[smem()] + [vmem()] * 3,
        out_specs=pl.BlockSpec(memory_space=pltpu.HBM),
        scratch_shapes=[
            pltpu.VMEM((PATCHES, wide) + tile, F32),
            pltpu.VMEM((classes, MOST_ACQ, row_total, cols), F32),
            pltpu.SemaphoreType.DMA((classes,)),
        ],
        compiler_params=params,
        name="merge",
    )(acq_counts, kept, lax.ppermute(send_a, "slab", pairs_a), lax.ppermute(send_b, "slab", pairs_b))


def solution(mesh):
    part = ("brain", "slab")
    in_specs = (P(None, part, None, None), P(), P(), P(), P(), P(), P(part, None), P(part, None), P(part))
    body = functools.partial(local, mesh.shape["slab"])
    return jax.shard_map(body, mesh=mesh, in_specs=in_specs, out_specs=P(None, part, None, None), check_vma=False)
```

```python
import functools
import jax
import jax.numpy as jnp
from jax import lax
from jax.experimental import pallas as pl
from jax.experimental.pallas import tpu as pltpu
from jax.sharding import PartitionSpec as P

PATCHES = 2
PATCH_ROWS = 8
MARGIN = 2
RIM = 4
PATCH_X = 10
MOST_ACQ = 8
PRIOR = 0.1
EPS = 1e-05
F32 = jnp.float32
BF16 = jnp.bfloat16
MIB = 1 << 20
UNIT = 32767.0


def vmem():
    return pl.BlockSpec(memory_space=pltpu.VMEM)


def smem():
    return pl.BlockSpec(memory_space=pltpu.SMEM)


def prep_kernel(*refs):
    small = (len(refs) - 3 - 2 - PATCHES) // 2
    feat, small_in, rest = refs[0], refs[1 : 1 + small], refs[1 + small :]
    (own, to_a), to_b, small_out = rest[:2], rest[2 : 2 + PATCHES], rest[2 + PATCHES : 2 + PATCHES + small]
    held, sems = rest[2 + PATCHES + small :]
    channels, planes, rows, cols = feat.shape
    copies = [pltpu.make_async_copy(feat.at[:, x], held.at[x], sems.at[x]) for x in range(planes)]
    copies += [pltpu.make_async_copy(a, b, sems.at[planes + i]) for i, (a, b) in enumerate(zip(small_in, small_out))]
    for copy in copies:
        copy.start()
    even = lax.rem(lax.axis_index("slab"), 2) == 0
    a_first = jnp.where(even, planes - RIM, 0)
    b_first = jnp.where(even, 0, planes - RIM)
    for x in range(planes):
        copies[x].wait()
        turned = jnp.swapaxes(held[x].astype(F32), 0, 1).astype(BF16)
        for p in range(PATCHES):
            own[p, x] = turned[p * PATCH_ROWS : (p + 1) * PATCH_ROWS]
    for p in range(PATCHES):
        to_a[p] = own[p, pl.ds(a_first, RIM)]
        to_b[p][...] = own[p, pl.ds(b_first, RIM)]
    for copy in copies[planes:]:
        copy.wait()


def column_of(table, folds, width):
    diag = lax.broadcasted_iota(jnp.int32, (width, width), 0) == lax.broadcasted_iota(jnp.int32, (width, width), 1)
    parts = []
    for f in range(folds):
        row = jnp.broadcast_to(table[f : f + 1, :], (width, width))
        parts.append(jnp.sum(jnp.where(diag, row, 0.0), axis=1, keepdims=True))
    return jnp.concatenate(parts, 0)


def head_tables(head_w, head_b, folds, classes, channels):
    rows, outs = classes * 2 * folds, folds * channels
    lane = lax.broadcasted_iota(jnp.int32, (channels, outs), 1)
    chan = lax.broadcasted_iota(jnp.int32, (channels, outs), 0)
    spread = (lane % channels == chan).astype(F32).astype(BF16)
    tall = []
    for k in range(classes):
        tall += [head_w[k].astype(F32)] * 2
    tall = jnp.concatenate(tall, 0).astype(BF16)
    table = jnp.dot(tall, spread, preferred_element_type=F32)
    row = lax.broadcasted_iota(jnp.int32, (rows, outs), 0)
    col = lax.broadcasted_iota(jnp.int32, (rows, outs), 1)
    table = jnp.where(row % folds == col // channels, table, 0.0).astype(BF16)
    row = lax.broadcasted_iota(jnp.int32, (rows, classes), 0)
    cls = lax.broadcasted_iota(jnp.int32, (rows, classes), 1)
    bias = jnp.zeros((rows, 1), F32)
    for f in range(folds):
        pick = (row // (2 * folds) == cls) & (row % folds == f)
        bias = bias + jnp.sum(jnp.where(pick, jnp.broadcast_to(head_b[f : f + 1, :], (rows, classes)), 0.0), axis=1, keepdims=True)
    return jnp.concatenate([table, table], 1), bias


def gauss(position, length):
    scaled = (position - (length - 1) / 2.0) / (length / 4.0)
    return jnp.exp(-0.5 * scaled * scaled)


def fill_taps(taps, plane, source):
    rows, channels, cols = source.shape
    lane = lax.broadcasted_iota(jnp.int32, (channels, cols), 1)
    for h in range(rows):
        value = source[h]
        wide = value.astype(F32)
        left = jnp.where(lane == 0, 0.0, pltpu.roll(wide, 1, 1)).astype(BF16)
        right = jnp.where(lane == cols - 1, 0.0, pltpu.roll(wide, cols - 1, 1)).astype(BF16)
        taps[plane, h + 1] = jnp.concatenate([left, value, right], 0)


def conv_plane(x, first, fresh, taps, w_all, conv, stats):
    zero_plane = taps.shape[0] - 1
    cols = taps.shape[-1]
    i = first + x
    below = jnp.where(x == 0, zero_plane, i - 1)
    above = jnp.where(x == PATCH_X - 1, zero_plane, i + 1)
    weights = w_all[...]
    for r in range(PATCH_ROWS // 2):
        halves = []
        for h in (r, r + PATCH_ROWS // 2):
            halves.append(jnp.concatenate([taps[t, h : h + 3].reshape(-1, cols) for t in (below, i, above)], 0))
        out = jnp.dot(weights, jnp.concatenate(halves, 1), preferred_element_type=F32)
        conv[x, r] = out
        one, two = out[:, :cols], out[:, cols:]
        base = stats[0]
        if fresh is not None and r == 0:
            base = jnp.where(fresh, 0.5 * (one + two), base)
            stats[0] = base
        one, two = one - base, two - base
        stats[1] += one + two
        stats[2] += one * one + two * two


def conv_planes(first, begin, end, fresh, *refs):
    def one_plane(x):
        conv_plane(x, first, x == begin if fresh else None, *refs)

    def two_planes(y, _):
        one_plane(begin + 2 * y)
        one_plane(begin + 2 * y + 1)
        return 0

    def last_plane(y, _):
        one_plane(end - 1)
        return 0

    total = end - begin
    lax.fori_loop(0, total // 2, two_planes, 0)
    lax.fori_loop(0, lax.rem(total, 2), last_plane, 0)


def patch_plan(offs, p, planes):
    even = lax.rem(lax.axis_index("slab"), 2) == 0
    first = RIM - MARGIN + offs[0, p]
    foreign = jnp.where(even, RIM - first, first + PATCH_X - RIM - planes)
    foreign = foreign + jnp.minimum(foreign, 1)
    return even, first, jnp.where(even, foreign, 0), jnp.where(even, PATCH_X, PATCH_X - foreign)


def pre_kernel(offs, own, from_a, wt, gain, nbias, head_w, head_b, taps0, taps1, conv0, stats0, w_all, head, hbias, scales):
    planes = own.shape[1]
    classes, folds, channels = head_w.shape
    outs = folds * channels
    cols = own.shape[-1]
    span = planes + 2 * RIM
    even = lax.rem(lax.axis_index("slab"), 2) == 0
    a_base = jnp.where(even, RIM + planes, 0)
    eye = (lax.broadcasted_iota(jnp.int32, (outs, outs), 0) == lax.broadcasted_iota(jnp.int32, (outs, outs), 1)).astype(F32).astype(BF16)
    wide_w = jnp.concatenate([wt[a] for a in range(3)], 0)
    w_all[...] = lax.dot_general(eye, wide_w, (((1,), (1,)), ((), ())), preferred_element_type=F32).astype(BF16)
    table, bias = head_tables(head_w, head_b, folds, classes, channels)
    head[...] = table
    hbias[...] = jnp.broadcast_to(bias, hbias.shape)
    scales[0] = jnp.broadcast_to(column_of(gain, folds, channels), (outs, cols))
    scales[1] = jnp.broadcast_to(column_of(nbias, folds, channels), (outs, cols))
    zero_row = jnp.zeros((3 * channels, cols), BF16)
    for p, taps in enumerate((taps0, taps1)):
        taps[span] = jnp.zeros(taps.shape[1:], BF16)

        def pad_rows(i, _):
            taps[i, 0] = zero_row
            taps[i, PATCH_ROWS + 1] = zero_row
            return 0

        def fill_own(i, _):
            fill_taps(taps, i + RIM, own.at[p, i])
            return 0

        def fill_a(i, _):
            fill_taps(taps, i + a_base, from_a.at[p, i])
            return 0

        lax.fori_loop(0, span, pad_rows, 0)
        lax.fori_loop(0, planes, fill_own, 0, unroll=2)
        lax.fori_loop(0, RIM, fill_a, 0, unroll=2)
    stats0[...] = jnp.zeros_like(stats0)
    _, first, begin, end = patch_plan(offs, 0, planes)
    conv_planes(first, begin, end, True, taps0, w_all, conv0, stats0)


def fill_b(even, from_b, taps):
    planes = taps.shape[0] - 1 - 2 * RIM
    base = jnp.where(even, 0, RIM + planes)

    def fill(i, _):
        fill_taps(taps, i + base, from_b.at[i])
        return 0

    lax.fori_loop(0, RIM, fill, 0, unroll=2)


def settle(stats, scales, norm):
    cols = stats.shape[-1]
    count = float(PATCH_X * PATCH_ROWS)
    total = stats[1] * (1.0 / count)
    spread = stats[2] - total * stats[1]
    lane_mean = stats[0] + total
    mean = jnp.mean(lane_mean, axis=1, keepdims=True)
    dev = lane_mean - mean
    var = jnp.sum(spread + count * dev * dev, axis=1, keepdims=True) * (1.0 / (count * cols))
    scale = lax.rsqrt(var + EPS) * scales[0]
    norm[0] = scale
    norm[1] = scales[1] - mean * scale


def clear_rest(first, placed):
    for q in range(placed.shape[0] - PATCH_X):
        placed[jnp.where(q < first, q, q + PATCH_X)] = jnp.zeros(placed.shape[1:], F32)


def finish_plane(x, first, keep, conv, norm, head, hbias, placed):
    classes, rows, cols = placed.shape[1:]
    folds = rows // 2
    sub = lax.broadcasted_iota(jnp.int32, (rows, cols), 0)
    lane = lax.broadcasted_iota(jnp.int32, (rows, cols), 1)
    lower = sub < folds
    scale, offset = (jnp.concatenate([norm[i], norm[i]], 1) for i in range(2))
    table = [[] for _ in range(classes)]
    for r in range(PATCH_ROWS // 2):
        act = conv[x, r] * scale + offset
        act = jnp.maximum(act, 0.01 * act)
        high = act.astype(BF16)
        low = (act - high.astype(F32)).astype(BF16)
        logits = jnp.dot(head[...], jnp.concatenate([high, low], 0), preferred_element_type=F32) + hbias[...]
        parts = []
        for k in range(classes):
            both = logits[k * rows : (k + 1) * rows]
            parts.append(jnp.where(lower, both[:, :cols], both[:, cols:]))
        top = functools.reduce(jnp.maximum, parts)
        parts = [jnp.exp(v - top) for v in parts]
        denom = 1.0 / functools.reduce(jnp.add, parts)
        for k in range(classes):
            table[k].append(parts[k] * denom)
    line = gauss(sub.astype(F32), PATCH_ROWS) * gauss(lane.astype(F32), cols)
    window = line * (gauss(jnp.full((rows, cols), x, jnp.int32).astype(F32), PATCH_X) * keep)
    odd = (sub % 2) == 1
    high_pair = (sub % 4) >= 2
    for k in range(classes):
        v = table[k]
        pairs = []
        for q in (0, 2):
            pairs.append(jnp.where(odd, v[q + 1] + pltpu.roll(v[q + 1], 1, 0), v[q] + pltpu.roll(v[q], 7, 0)))
        full = jnp.where(high_pair, pairs[1] + pltpu.roll(pairs[1], 2, 0), pairs[0] + pltpu.roll(pairs[0], 6, 0))
        placed[first + x, k] = full * window


def mid_kernel(offs, mask, from_b, taps0_in, conv0_in, stats0_in, taps1, w_all, head, hbias, scales, placed, norm, conv1, stats1, taps0, conv0, stats0):
    planes = taps0.shape[0] - 1 - 2 * RIM
    folds = placed.shape[2] // 2
    even, first0, begin, end = patch_plan(offs, 0, planes)
    fill_b(even, from_b, taps0)
    conv_planes(first0, jnp.where(even, 0, end), jnp.where(even, begin, PATCH_X), False, taps0, w_all, conv0, stats0)
    settle(stats0, scales, norm)
    clear_rest(first0, placed)
    stats1[...] = jnp.zeros_like(stats1)
    keep = mask[0, 0].astype(F32) * (1.0 / folds)
    _, first1, begin, end = patch_plan(offs, 1, planes)

    def both(y, _):
        finish_plane(y, first0, keep, conv0, norm, head, hbias, placed)
        conv_plane(begin + y, first1, y == 0, taps1, w_all, conv1, stats1)
        return 0

    lax.fori_loop(0, end - begin, both, 0)


def post_kernel(offs, mask, from_b, conv0, norm0, w_all, head, hbias, scales, taps1_in, conv1_in, stats1_in, placed0_in, placed0, placed1, to_a, to_b, taps1, conv1, stats1, norm1):
    planes = taps1.shape[0] - 1 - 2 * RIM
    folds = placed1.shape[2] // 2
    even, first0, _, _ = patch_plan(offs, 0, planes)
    _, first1, begin, end = patch_plan(offs, 1, planes)
    fill_b(even, from_b, taps1)
    keep0, keep1 = (mask[0, p].astype(F32) * (1.0 / folds) for p in range(PATCHES))
    done = end - begin
    waiting = jnp.where(even, 0, end)

    def both(y, _):
        finish_plane(done + y, first0, keep0, conv0, norm0, head, hbias, placed0)
        conv_plane(waiting + y, first1, None, taps1, w_all, conv1, stats1)
        return 0

    lax.fori_loop(0, PATCH_X - done, both, 0)
    settle(stats1, scales, norm1)
    clear_rest(first1, placed1)

    def finish(x, _):
        finish_plane(x, first1, keep1, conv1, norm1, head, hbias, placed1)
        return 0

    lax.fori_loop(0, PATCH_X, finish, 0, unroll=2)
    for send, begin in ((to_a, jnp.where(even, planes + RIM - 1, 0)), (to_b, jnp.where(even, 0, planes + RIM - 1))):
        for p, placed in enumerate((placed0, placed1)):
            for j in range(RIM + 1):
                send[p, j] = (placed[begin + j] * UNIT + 0.5).astype(jnp.int32).astype(jnp.int16)


def merge_kernel(slabs, acq, placed0, placed1, from_a, from_b, out, merged, held, sems):
    planes = placed0.shape[0] - 2 * RIM
    wide = planes + 2
    classes, rows, cols = placed0.shape[1:]
    slab = lax.axis_index("slab")
    even = lax.rem(slab, 2) == 0
    a_base = jnp.where(even, wide - RIM - 1, 0)
    b_base = jnp.where(even, 0, wide - RIM - 1)
    shape = (rows, cols)
    count = jnp.full(shape, acq[0], jnp.int32).astype(F32)
    anchor = jnp.full(shape, slab * planes, jnp.int32).astype(F32)
    step = planes / jnp.maximum(count - 1.0, 1.0)
    for p, placed in enumerate((placed0, placed1)):
        merged[p] = placed[RIM - 1 : RIM - 1 + wide]
        for base, got in ((a_base, from_a), (b_base, from_b)):
            for j in range(RIM + 1):
                merged[p, base + j] += got[p, j].astype(jnp.int32).astype(F32) * (1.0 / UNIT)
        for j in range(wide):
            parts = [merged[p, j, k] for k in range(classes)]
            scale = 1.0 / (functools.reduce(jnp.add, parts) + PRIOR)
            parts[0] = parts[0] + PRIOR
            for k in range(classes):
                merged[p, j, k] = parts[k] * scale
    gains = []
    for s in range(MOST_ACQ):
        place = jnp.clip(anchor + (s * step - 0.5), 0.0, float(slabs * planes - 1)) - anchor
        used = (s < count).astype(F32)
        gains.append([jnp.maximum(0.0, 1.0 - jnp.abs(place - (j - 1.0))) * used for j in range(wide)])
    copies = []
    for k in range(classes):
        for p in range(PATCHES):
            column = [merged[p, j, k] for j in range(wide)]
            for s in range(MOST_ACQ):
                held[k, s, p * rows : (p + 1) * rows] = functools.reduce(jnp.add, [g * v for g, v in zip(gains[s], column)])
        copies.append(pltpu.make_async_copy(held.at[k], out.at[k], sems.at[k]))
        copies[-1].start()
    for copy in copies:
        copy.wait()


def local(slabs, features, conv_weight, norm_gain, norm_bias, head_weight, head_bias, patch_offsets, fg_mask, acq_counts):
    channels, planes, row_total, cols = features.shape
    folds, classes, _ = head_weight.shape
    outs = folds * channels
    pairs_a = [(i, i ^ 1) for i in range(slabs) if (i ^ 1) < slabs]
    pairs_b = [(i, ((i + 1) ^ 1) - 1) for i in range(slabs) if 0 <= ((i + 1) ^ 1) - 1 < slabs]
    shaped = jax.ShapeDtypeStruct
    cell = (PATCH_ROWS, channels, cols)
    params = pltpu.CompilerParams(vmem_limit_bytes=24 * MIB)
    small = [jnp.swapaxes(conv_weight, 1, 2), norm_gain, norm_bias, jnp.swapaxes(head_weight, 0, 1), head_bias, patch_offsets, fg_mask]
    own, to_a, *rest = pl.pallas_call(
        prep_kernel,
        out_shape=[shaped((PATCHES, planes) + cell, BF16), shaped((PATCHES, RIM) + cell, BF16)]
        + [shaped((RIM,) + cell, BF16)] * PATCHES
        + [shaped(v.shape, v.dtype) for v in small],
        in_specs=[pl.BlockSpec(memory_space=pltpu.HBM)] * (1 + len(small)),
        out_specs=[vmem()] * (2 + PATCHES + len(small)),
        scratch_shapes=[pltpu.VMEM((planes, channels, row_total, cols), BF16), pltpu.SemaphoreType.DMA((planes + len(small),))],
        compiler_params=params,
        name="prep",
    )(*[pltpu.with_memory_space_constraint(v, pltpu.HBM) for v in (features, *small)])
    to_b, (conv_weight, norm_gain, norm_bias, head_weight, head_bias, patch_offsets, fg_mask) = rest[:PATCHES], rest[PATCHES:]
    from_a = lax.ppermute(to_a, "slab", pairs_a)
    from_b = [lax.ppermute(v, "slab", pairs_b) for v in to_b]
    wide = planes + 2
    tile = (classes, PATCH_ROWS, cols)
    span = planes + 2 * RIM
    taps_shape = shaped((span + 1, PATCH_ROWS + 2, 3 * channels, cols), BF16)
    conv_shape = shaped((PATCH_X, PATCH_ROWS // 2, outs, 2 * cols), F32)
    stats_shape = shaped((3, outs, cols), F32)
    table_shapes = [shaped((outs, 27 * channels), BF16), shaped((classes * 2 * folds, 2 * outs), BF16), shaped((classes * 2 * folds, 2 * cols), F32), shaped((2, outs, cols), F32)]
    placed_shape = shaped((span,) + tile, F32)
    norm_shape = shaped((2, outs, cols), F32)
    send_shape = shaped((PATCHES, RIM + 1) + tile, jnp.int16)
    taps0, taps1, conv0, stats0, *tables = pl.pallas_call(
        pre_kernel,
        out_shape=[taps_shape, taps_shape, conv_shape, stats_shape] + table_shapes,
        in_specs=[smem()] + [vmem()] * 7,
        out_specs=[vmem()] * 8,
        compiler_params=params,
        name="pre",
    )(patch_offsets, own, from_a, conv_weight, norm_gain, norm_bias, head_weight, head_bias)
    placed0, norm0, conv1, stats1, _, conv0, _ = pl.pallas_call(
        mid_kernel,
        out_shape=[placed_shape, norm_shape, conv_shape, stats_shape, taps_shape, conv_shape, stats_shape],
        in_specs=[smem()] * 2 + [vmem()] * 9,
        out_specs=[vmem()] * 7,
        input_output_aliases={3: 4, 4: 5, 5: 6},
        compiler_params=params,
        name="mid",
    )(patch_offsets, fg_mask, from_b[0], taps0, conv0, stats0, taps1, *tables)
    placed0, placed1, send_a, send_b, *_ = pl.pallas_call(
        post_kernel,
        out_shape=[placed_shape, placed_shape, send_shape, send_shape, taps_shape, conv_shape, stats_shape],
        in_specs=[smem()] * 2 + [vmem()] * 11,
        out_specs=[vmem()] * 7,
        input_output_aliases={12: 0, 9: 4, 10: 5, 11: 6},
        scratch_shapes=[pltpu.VMEM(norm_shape.shape, F32)],
        compiler_params=params,
        name="post",
    )(patch_offsets, fg_mask, from_b[1], conv0, norm0, *tables, taps1, conv1, stats1, placed0)
    return pl.pallas_call(
        functools.partial(merge_kernel, slabs),
        out_shape=shaped((classes, MOST_ACQ, row_total, cols), F32),
        in_specs=[smem()] + [vmem()] * 4,
        out_specs=pl.BlockSpec(memory_space=pltpu.HBM),
        scratch_shapes=[
            pltpu.VMEM((PATCHES, wide) + tile, F32),
            pltpu.VMEM((classes, MOST_ACQ, row_total, cols), F32),
            pltpu.SemaphoreType.DMA((classes,)),
        ],
        compiler_params=params,
        name="merge",
    )(acq_counts, placed0, placed1, lax.ppermute(send_a, "slab", pairs_a), lax.ppermute(send_b, "slab", pairs_b))


def solution(mesh):
    part = ("brain", "slab")
    in_specs = (P(None, part, None, None), P(), P(), P(), P(), P(), P(part, None), P(part, None), P(part))
    body = functools.partial(local, mesh.shape["slab"])
    return jax.shard_map(body, mesh=mesh, in_specs=in_specs, out_specs=P(None, part, None, None), check_vma=False)
```

```python
import functools
import jax
import jax.numpy as jnp
from jax import lax
from jax.experimental import pallas as pl
from jax.experimental.pallas import tpu as pltpu
from jax.sharding import PartitionSpec as P

PATCHES = 2
PATCH_ROWS = 8
MARGIN = 2
RIM = 4
PATCH_X = 10
MOST_ACQ = 8
PRIOR = 0.1
EPS = 1e-05
F32 = jnp.float32
BF16 = jnp.bfloat16
MIB = 1 << 20
GROUP = 5
UNIT = 32767.0


def vmem():
    return pl.BlockSpec(memory_space=pltpu.VMEM)


def smem():
    return pl.BlockSpec(memory_space=pltpu.SMEM)


def prep_kernel(*refs):
    small = (len(refs) - 3 - 3) // 2
    feat, small_in, rest = refs[0], refs[1 : 1 + small], refs[1 + small :]
    (own, to_a, to_b), small_out, (held, sems) = rest[:3], rest[3 : 3 + small], rest[3 + small :]
    channels, planes, rows, cols = feat.shape
    copies = [pltpu.make_async_copy(feat.at[:, x], held.at[x], sems.at[x]) for x in range(planes)]
    copies += [pltpu.make_async_copy(a, b, sems.at[planes + i]) for i, (a, b) in enumerate(zip(small_in, small_out))]
    for copy in copies:
        copy.start()
    even = lax.rem(lax.axis_index("slab"), 2) == 0
    a_first = jnp.where(even, planes - RIM, 0)
    b_first = jnp.where(even, 0, planes - RIM)
    for x in range(planes):
        copies[x].wait()
        turned = jnp.swapaxes(held[x].astype(F32), 0, 1).astype(BF16)
        for p in range(PATCHES):
            own[p, x] = turned[p * PATCH_ROWS : (p + 1) * PATCH_ROWS]
    to_b[...] = own[0, pl.ds(b_first, RIM)]
    for p in range(PATCHES):
        to_a[p] = own[p, pl.ds(a_first, RIM)]
    for copy in copies[planes:]:
        copy.wait()


def column_of(table, folds, width):
    diag = lax.broadcasted_iota(jnp.int32, (width, width), 0) == lax.broadcasted_iota(jnp.int32, (width, width), 1)
    parts = []
    for f in range(folds):
        row = jnp.broadcast_to(table[f : f + 1, :], (width, width))
        parts.append(jnp.sum(jnp.where(diag, row, 0.0), axis=1, keepdims=True))
    return jnp.concatenate(parts, 0)


def head_tables(head_w, head_b, folds, classes, channels):
    rows, outs = classes * 2 * folds, folds * channels
    lane = lax.broadcasted_iota(jnp.int32, (channels, outs), 1)
    chan = lax.broadcasted_iota(jnp.int32, (channels, outs), 0)
    spread = (lane % channels == chan).astype(F32).astype(BF16)
    tall = []
    for k in range(classes):
        tall += [head_w[k].astype(F32)] * 2
    tall = jnp.concatenate(tall, 0).astype(BF16)
    table = jnp.dot(tall, spread, preferred_element_type=F32)
    row = lax.broadcasted_iota(jnp.int32, (rows, outs), 0)
    col = lax.broadcasted_iota(jnp.int32, (rows, outs), 1)
    table = jnp.where(row % folds == col // channels, table, 0.0).astype(BF16)
    row = lax.broadcasted_iota(jnp.int32, (rows, classes), 0)
    cls = lax.broadcasted_iota(jnp.int32, (rows, classes), 1)
    bias = jnp.zeros((rows, 1), F32)
    for f in range(folds):
        pick = (row // (2 * folds) == cls) & (row % folds == f)
        bias = bias + jnp.sum(jnp.where(pick, jnp.broadcast_to(head_b[f : f + 1, :], (rows, classes)), 0.0), axis=1, keepdims=True)
    return jnp.concatenate([table, table], 1), bias


def gauss(position, length):
    scaled = (position - (length - 1) / 2.0) / (length / 4.0)
    return jnp.exp(-0.5 * scaled * scaled)


def fill_taps(taps, plane, source):
    rows, channels, cols = source.shape
    lane = lax.broadcasted_iota(jnp.int32, (channels, cols), 1)
    not_first = (lane != 0).astype(F32).astype(BF16)
    not_last = (lane != cols - 1).astype(F32).astype(BF16)
    for h in range(rows):
        value = source[h]
        left = pltpu.roll(value, 1, 1) * not_first
        right = pltpu.roll(value, cols - 1, 1) * not_last
        taps[plane, h + 1] = jnp.concatenate([left, value, right], 0)


def run(*steps):
    steps = list(steps)
    while steps:
        for step in list(steps):
            try:
                next(step)
            except StopIteration:
                steps.remove(step)


def conv_plane(x, first, fresh, taps, w_all, conv, stats):
    zero_plane = taps.shape[0] - 1
    cols = taps.shape[-1]
    i = first + x
    below = jnp.where(x == 0, zero_plane, i - 1)
    above = jnp.where(x == PATCH_X - 1, zero_plane, i + 1)
    weights = w_all[...]
    for r in range(PATCH_ROWS // 2):
        halves = []
        for h in (r, r + PATCH_ROWS // 2):
            halves.append(jnp.concatenate([taps[t, h : h + 3].reshape(-1, cols) for t in (below, i, above)], 0))
        out = jnp.dot(weights, jnp.concatenate(halves, 1), preferred_element_type=F32)
        conv[x, r] = out
        one, two = out[:, :cols], out[:, cols:]
        base = stats[0]
        if fresh is not None and r == 0:
            base = jnp.where(fresh, 0.5 * (one + two), base)
            stats[0] = base
        one, two = one - base, two - base
        stats[1] += one + two
        stats[2] += one * one + two * two
        yield


def conv_planes(first, begin, end, fresh, *refs):
    def one_plane(x):
        run(conv_plane(x, first, x == begin if fresh else None, *refs))

    def last_plane(y, _):
        one_plane(end - 1)
        return 0

    def many_planes(y, _):
        for d in range(GROUP):
            one_plane(begin + GROUP * y + d)
        return 0

    total = end - begin
    groups = total // GROUP
    left = lax.rem(total, GROUP)
    lax.fori_loop(0, groups, many_planes, 0)
    begin_left = begin + GROUP * groups

    def two_planes(y, _):
        one_plane(begin_left + 2 * y)
        one_plane(begin_left + 2 * y + 1)
        return 0

    lax.fori_loop(0, left // 2, two_planes, 0)
    lax.fori_loop(0, lax.rem(left, 2), last_plane, 0)


def patch_plan(offs, p, planes):
    even = lax.rem(lax.axis_index("slab"), 2) == 0
    first = RIM - MARGIN + offs[0, p]
    foreign = jnp.where(even, RIM - first, first + PATCH_X - RIM - planes)
    foreign = foreign + jnp.minimum(foreign, 1)
    return even, first, jnp.where(even, foreign, 0), jnp.where(even, PATCH_X, PATCH_X - foreign)


def pre_kernel(offs, own, from_a, wt, gain, nbias, head_w, head_b, to_b, taps0, taps1, conv0, stats0, w_all, head, hbias, scales):
    planes = own.shape[1]
    classes, folds, channels = head_w.shape
    outs = folds * channels
    cols = own.shape[-1]
    span = planes + 2 * RIM
    even = lax.rem(lax.axis_index("slab"), 2) == 0
    a_base = jnp.where(even, RIM + planes, 0)
    to_b[...] = own[1, pl.ds(jnp.where(even, 0, planes - RIM), RIM)]
    eye = (lax.broadcasted_iota(jnp.int32, (outs, outs), 0) == lax.broadcasted_iota(jnp.int32, (outs, outs), 1)).astype(F32).astype(BF16)
    wide_w = jnp.concatenate([wt[a] for a in range(3)], 0)
    w_all[...] = lax.dot_general(eye, wide_w, (((1,), (1,)), ((), ())), preferred_element_type=F32).astype(BF16)
    table, bias = head_tables(head_w, head_b, folds, classes, channels)
    head[...] = table
    hbias[...] = jnp.broadcast_to(bias, hbias.shape)
    scales[0] = jnp.broadcast_to(column_of(gain, folds, channels), (outs, cols))
    scales[1] = jnp.broadcast_to(column_of(nbias, folds, channels), (outs, cols))
    zero_row = jnp.zeros((3 * channels, cols), BF16)
    for p, taps in enumerate((taps0, taps1)):
        taps[span] = jnp.zeros(taps.shape[1:], BF16)

        def pad_rows(i, _):
            taps[i, 0] = zero_row
            taps[i, PATCH_ROWS + 1] = zero_row
            return 0

        def fill_own(i, _):
            fill_taps(taps, i + RIM, own.at[p, i])
            return 0

        def fill_a(i, _):
            fill_taps(taps, i + a_base, from_a.at[p, i])
            return 0

        lax.fori_loop(0, span, pad_rows, 0)
        lax.fori_loop(0, planes, fill_own, 0, unroll=2)
        lax.fori_loop(0, RIM, fill_a, 0, unroll=2)
    stats0[...] = jnp.zeros_like(stats0)
    _, first, begin, end = patch_plan(offs, 0, planes)
    conv_planes(first, begin, end, True, taps0, w_all, conv0, stats0)


def fill_b(even, from_b, taps):
    planes = taps.shape[0] - 1 - 2 * RIM
    base = jnp.where(even, 0, RIM + planes)

    def fill(i, _):
        fill_taps(taps, i + base, from_b.at[i])
        return 0

    lax.fori_loop(0, RIM, fill, 0, unroll=2)


def settle(stats, scales, norm):
    cols = stats.shape[-1]
    count = float(PATCH_X * PATCH_ROWS)
    total = stats[1] * (1.0 / count)
    spread = stats[2] - total * stats[1]
    lane_mean = stats[0] + total
    mean = jnp.mean(lane_mean, axis=1, keepdims=True)
    dev = lane_mean - mean
    var = jnp.sum(spread + count * dev * dev, axis=1, keepdims=True) * (1.0 / (count * cols))
    scale = lax.rsqrt(var + EPS) * scales[0]
    norm[0] = scale
    norm[1] = scales[1] - mean * scale


def clear_rest(first, placed):
    for q in range(placed.shape[0] - PATCH_X):
        placed[jnp.where(q < first, q, q + PATCH_X)] = jnp.zeros(placed.shape[1:], F32)


def finish_plane(x, first, keep, conv, norm, head, hbias, placed):
    classes, rows, cols = placed.shape[1:]
    folds = rows // 2
    sub = lax.broadcasted_iota(jnp.int32, (rows, cols), 0)
    lane = lax.broadcasted_iota(jnp.int32, (rows, cols), 1)
    lower = sub < folds
    scale, offset = (jnp.concatenate([norm[i], norm[i]], 1) for i in range(2))
    table = [[] for _ in range(classes)]
    for r in range(PATCH_ROWS // 2):
        act = conv[x, r] * scale + offset
        act = jnp.maximum(act, 0.01 * act)
        high = act.astype(BF16)
        low = (act - high.astype(F32)).astype(BF16)
        logits = jnp.dot(head[...], jnp.concatenate([high, low], 0), preferred_element_type=F32) + hbias[...]
        parts = []
        for k in range(classes):
            both = logits[k * rows : (k + 1) * rows]
            parts.append(jnp.where(lower, both[:, :cols], both[:, cols:]))
        top = functools.reduce(jnp.maximum, parts)
        parts = [jnp.exp(v - top) for v in parts]
        denom = 1.0 / functools.reduce(jnp.add, parts)
        for k in range(classes):
            table[k].append(parts[k] * denom)
        yield
    line = gauss(sub.astype(F32), PATCH_ROWS) * gauss(lane.astype(F32), cols)
    window = line * (gauss(jnp.full((rows, cols), x, jnp.int32).astype(F32), PATCH_X) * keep)
    odd = (sub % 2) == 1
    high_pair = (sub % 4) >= 2
    for k in range(classes):
        v = table[k]
        pairs = []
        for q in (0, 2):
            pairs.append(jnp.where(odd, v[q + 1] + pltpu.roll(v[q + 1], 1, 0), v[q] + pltpu.roll(v[q], 7, 0)))
        full = jnp.where(high_pair, pairs[1] + pltpu.roll(pairs[1], 2, 0), pairs[0] + pltpu.roll(pairs[0], 6, 0))
        placed[first + x, k] = full * window


def mid_kernel(offs, mask, from_b, taps0_in, conv0_in, stats0_in, taps1, w_all, head, hbias, scales, placed, norm, conv1, stats1, taps0, conv0, stats0):
    planes = taps0.shape[0] - 1 - 2 * RIM
    folds = placed.shape[2] // 2
    even, first0, begin, end = patch_plan(offs, 0, planes)
    fill_b(even, from_b, taps0)
    conv_planes(first0, jnp.where(even, 0, end), jnp.where(even, begin, PATCH_X), False, taps0, w_all, conv0, stats0)
    settle(stats0, scales, norm)
    clear_rest(first0, placed)
    stats1[...] = jnp.zeros_like(stats1)
    keep = mask[0, 0].astype(F32) * (1.0 / folds)
    _, first1, begin, end = patch_plan(offs, 1, planes)

    def both(y, _):
        run(conv_plane(begin + y, first1, y == 0, taps1, w_all, conv1, stats1), finish_plane(y, first0, keep, conv0, norm, head, hbias, placed))
        return 0

    def both_twice(y, _):
        both(2 * y, 0)
        both(2 * y + 1, 0)
        return 0

    lax.fori_loop(0, (end - begin) // 2, both_twice, 0)
    lax.fori_loop((end - begin) // 2 * 2, end - begin, both, 0)


def post_kernel(offs, mask, from_b, conv0, norm0, w_all, head, hbias, scales, taps1_in, conv1_in, stats1_in, placed0_in, placed0, placed1, to_a, to_b, taps1, conv1, stats1, norm1):
    planes = taps1.shape[0] - 1 - 2 * RIM
    folds = placed1.shape[2] // 2
    even, first0, _, _ = patch_plan(offs, 0, planes)
    _, first1, begin, end = patch_plan(offs, 1, planes)
    fill_b(even, from_b, taps1)
    keep0, keep1 = (mask[0, p].astype(F32) * (1.0 / folds) for p in range(PATCHES))
    done = end - begin
    waiting = jnp.where(even, 0, end)

    def both(y, _):
        run(conv_plane(waiting + y, first1, None, taps1, w_all, conv1, stats1), finish_plane(done + y, first0, keep0, conv0, norm0, head, hbias, placed0))
        return 0

    def both_twice(y, _):
        both(2 * y, 0)
        both(2 * y + 1, 0)
        return 0

    left = PATCH_X - done
    lax.fori_loop(0, left // 2, both_twice, 0)
    lax.fori_loop(left // 2 * 2, left, both, 0)
    settle(stats1, scales, norm1)
    clear_rest(first1, placed1)

    def finish(x, _):
        run(finish_plane(x, first1, keep1, conv1, norm1, head, hbias, placed1))
        return 0

    lax.fori_loop(0, PATCH_X, finish, 0, unroll=5)
    for send, begin in ((to_a, jnp.where(even, planes + RIM - 1, 0)), (to_b, jnp.where(even, 0, planes + RIM - 1))):
        for p, placed in enumerate((placed0, placed1)):
            for j in range(RIM + 1):
                send[p, j] = (placed[begin + j] * UNIT + 0.5).astype(jnp.int32).astype(jnp.int16)


def gather_kernel(placed0, placed1, from_a, summed):
    planes = placed0.shape[0] - 2 * RIM
    wide = planes + 2
    even = lax.rem(lax.axis_index("slab"), 2) == 0
    base = jnp.where(even, wide - RIM - 1, 0)
    for p, placed in enumerate((placed0, placed1)):
        summed[p] = placed[RIM - 1 : RIM - 1 + wide]
        for j in range(RIM + 1):
            summed[p, base + j] += from_a[p, j].astype(jnp.int32).astype(F32) * (1.0 / UNIT)


def merge_kernel(slabs, acq, summed, from_b, out, merged, held, sems):
    wide = summed.shape[1]
    planes = wide - 2
    classes, rows, cols = summed.shape[2:]
    slab = lax.axis_index("slab")
    even = lax.rem(slab, 2) == 0
    base = jnp.where(even, 0, wide - RIM - 1)
    shape = (rows, cols)
    gaps = jnp.maximum(acq[0] - 1, 1)
    count = jnp.full(shape, acq[0], jnp.int32).astype(F32)
    anchor = jnp.full(shape, slab * planes, jnp.int32).astype(F32)
    step = planes / jnp.maximum(count - 1.0, 1.0)
    lowest = jnp.where(slab == 0, 0, -1)
    firsts, gains = [], []
    for s in range(MOST_ACQ):
        first = lax.div(2 * planes * s + gaps, 2 * gaps) - 1
        first = jnp.minimum(jnp.maximum(first, lowest), planes - 1)
        place = jnp.clip(anchor + (s * step - 0.5), 0.0, float(slabs * planes - 1)) - anchor
        used = (s < count).astype(F32)
        near = place - jnp.full(shape, first, jnp.int32).astype(F32)
        firsts.append(first + 1)
        gains.append([jnp.maximum(0.0, 1.0 - jnp.abs(near - d)) * used for d in range(2)])
    for p in range(PATCHES):
        merged[p] = summed[p]
        for j in range(RIM + 1):
            merged[p, base + j] += from_b[p, j].astype(jnp.int32).astype(F32) * (1.0 / UNIT)
        for j in range(wide):
            parts = [merged[p, j, k] for k in range(classes)]
            scale = 1.0 / (functools.reduce(jnp.add, parts) + PRIOR)
            parts[0] = parts[0] + PRIOR
            for k in range(classes):
                merged[p, j, k] = parts[k] * scale
    copies = []
    for k in range(classes):
        for p in range(PATCHES):
            for s in range(MOST_ACQ):
                held[k, s, p * rows : (p + 1) * rows] = gains[s][0] * merged[p, firsts[s], k] + gains[s][1] * merged[p, firsts[s] + 1, k]
        copies.append(pltpu.make_async_copy(held.at[k], out.at[k], sems.at[k]))
        copies[-1].start()
    for copy in copies:
        copy.wait()


def local(slabs, features, conv_weight, norm_gain, norm_bias, head_weight, head_bias, patch_offsets, fg_mask, acq_counts):
    channels, planes, row_total, cols = features.shape
    folds, classes, _ = head_weight.shape
    outs = folds * channels
    pairs_a = [(i, i ^ 1) for i in range(slabs) if (i ^ 1) < slabs]
    pairs_b = [(i, ((i + 1) ^ 1) - 1) for i in range(slabs) if 0 <= ((i + 1) ^ 1) - 1 < slabs]
    shaped = jax.ShapeDtypeStruct
    cell = (PATCH_ROWS, channels, cols)
    halo_shape = shaped((RIM,) + cell, BF16)
    params = pltpu.CompilerParams(vmem_limit_bytes=24 * MIB)
    small = [jnp.swapaxes(conv_weight, 1, 2), norm_gain, norm_bias, jnp.swapaxes(head_weight, 0, 1), head_bias, patch_offsets, fg_mask]
    own, to_a, *rest = pl.pallas_call(
        prep_kernel,
        out_shape=[shaped((PATCHES, planes) + cell, BF16), shaped((PATCHES, RIM) + cell, BF16)]
        + [halo_shape]
        + [shaped(v.shape, v.dtype) for v in small],
        in_specs=[pl.BlockSpec(memory_space=pltpu.HBM)] * (1 + len(small)),
        out_specs=[vmem()] * (3 + len(small)),
        scratch_shapes=[pltpu.VMEM((planes, channels, row_total, cols), BF16), pltpu.SemaphoreType.DMA((planes + len(small),))],
        compiler_params=params,
        name="prep",
    )(*[pltpu.with_memory_space_constraint(v, pltpu.HBM) for v in (features, *small)])
    to_b, conv_weight, norm_gain, norm_bias, head_weight, head_bias, patch_offsets, fg_mask = rest
    from_a = lax.ppermute(to_a, "slab", pairs_a)
    from_b0 = lax.ppermute(to_b, "slab", pairs_b)
    wide = planes + 2
    tile = (classes, PATCH_ROWS, cols)
    span = planes + 2 * RIM
    taps_shape = shaped((span + 1, PATCH_ROWS + 2, 3 * channels, cols), BF16)
    conv_shape = shaped((PATCH_X, PATCH_ROWS // 2, outs, 2 * cols), F32)
    stats_shape = shaped((3, outs, cols), F32)
    table_shapes = [shaped((outs, 27 * channels), BF16), shaped((classes * 2 * folds, 2 * outs), BF16), shaped((classes * 2 * folds, 2 * cols), F32), shaped((2, outs, cols), F32)]
    placed_shape = shaped((span,) + tile, F32)
    norm_shape = shaped((2, outs, cols), F32)
    send_shape = shaped((PATCHES, RIM + 1) + tile, jnp.int16)
    to_b, taps0, taps1, conv0, stats0, *tables = pl.pallas_call(
        pre_kernel,
        out_shape=[halo_shape, taps_shape, taps_shape, conv_shape, stats_shape] + table_shapes,
        in_specs=[smem()] + [vmem()] * 7,
        out_specs=[vmem()] * 9,
        compiler_params=params,
        name="pre",
    )(patch_offsets, own, from_a, conv_weight, norm_gain, norm_bias, head_weight, head_bias)
    placed0, norm0, conv1, stats1, _, conv0, _ = pl.pallas_call(
        mid_kernel,
        out_shape=[placed_shape, norm_shape, conv_shape, stats_shape, taps_shape, conv_shape, stats_shape],
        in_specs=[smem()] * 2 + [vmem()] * 9,
        out_specs=[vmem()] * 7,
        input_output_aliases={3: 4, 4: 5, 5: 6},
        compiler_params=params,
        name="mid",
    )(patch_offsets, fg_mask, from_b0, taps0, conv0, stats0, taps1, *tables)
    from_b1 = lax.ppermute(to_b, "slab", pairs_b)
    placed0, placed1, send_a, send_b, *_ = pl.pallas_call(
        post_kernel,
        out_shape=[placed_shape, placed_shape, send_shape, send_shape, taps_shape, conv_shape, stats_shape],
        in_specs=[smem()] * 2 + [vmem()] * 11,
        out_specs=[vmem()] * 7,
        input_output_aliases={12: 0, 9: 4, 10: 5, 11: 6},
        scratch_shapes=[pltpu.VMEM(norm_shape.shape, F32)],
        compiler_params=params,
        name="post",
    )(patch_offsets, fg_mask, from_b1, conv0, norm0, *tables, taps1, conv1, stats1, placed0)
    got_a = lax.ppermute(send_a, "slab", pairs_a)
    got_b = lax.ppermute(send_b, "slab", pairs_b)
    summed = pl.pallas_call(
        gather_kernel,
        out_shape=shaped((PATCHES, wide) + tile, F32),
        in_specs=[vmem()] * 3,
        out_specs=vmem(),
        compiler_params=params,
        name="gather",
    )(placed0, placed1, got_a)
    return pl.pallas_call(
        functools.partial(merge_kernel, slabs),
        out_shape=shaped((classes, MOST_ACQ, row_total, cols), F32),
        in_specs=[smem()] + [vmem()] * 2,
        out_specs=pl.BlockSpec(memory_space=pltpu.HBM),
        scratch_shapes=[
            pltpu.VMEM((PATCHES, wide) + tile, F32),
            pltpu.VMEM((classes, MOST_ACQ, row_total, cols), F32),
            pltpu.SemaphoreType.DMA((classes,)),
        ],
        compiler_params=params,
        name="merge",
    )(acq_counts, summed, got_b)


def solution(mesh):
    part = ("brain", "slab")
    in_specs = (P(None, part, None, None), P(), P(), P(), P(), P(), P(part, None), P(part, None), P(part))
    body = functools.partial(local, mesh.shape["slab"])
    return jax.shard_map(body, mesh=mesh, in_specs=in_specs, out_specs=P(None, part, None, None), check_vma=False)
```

```python
import functools
import jax
import jax.numpy as jnp
from jax import lax
from jax.experimental import pallas as pl
from jax.experimental.pallas import tpu as pltpu
from jax.sharding import PartitionSpec as P

PATCHES = 2
PATCH_ROWS = 8
MARGIN = 2
RIM = 4
PATCH_X = 10
MOST_ACQ = 8
PRIOR = 0.1
EPS = 1e-05
F32 = jnp.float32
BF16 = jnp.bfloat16
MIB = 1 << 20
GROUP = 5
UNIT = 32767.0


def vmem():
    return pl.BlockSpec(memory_space=pltpu.VMEM)


def smem():
    return pl.BlockSpec(memory_space=pltpu.SMEM)


def prep_kernel(*refs):
    small = (len(refs) - 7) // 2
    feat, small_in, rest = refs[0], refs[1 : 1 + small], refs[1 + small :]
    (own, to_a, *to_b), small_out, (held, sems) = rest[:4], rest[4 : 4 + small], rest[4 + small :]
    channels, planes, rows, cols = feat.shape
    copies = [pltpu.make_async_copy(feat.at[:, x], held.at[x], sems.at[x]) for x in range(planes)]
    copies += [pltpu.make_async_copy(a, b, sems.at[planes + i]) for i, (a, b) in enumerate(zip(small_in, small_out))]
    for copy in copies:
        copy.start()
    even = lax.rem(lax.axis_index("slab"), 2) == 0
    a_first = jnp.where(even, planes - RIM, 0)
    b_first = jnp.where(even, 0, planes - RIM)
    for x in range(planes):
        copies[x].wait()
        turned = jnp.swapaxes(held[x].astype(F32), 0, 1).astype(BF16)
        for p in range(PATCHES):
            own[p, x] = turned[p * PATCH_ROWS : (p + 1) * PATCH_ROWS]
    for p in range(PATCHES):
        to_a[p] = own[p, pl.ds(a_first, RIM)]
        to_b[p][...] = own[p, pl.ds(b_first, RIM)]
    for copy in copies[planes:]:
        copy.wait()


def column_of(table, folds, width):
    diag = lax.broadcasted_iota(jnp.int32, (width, width), 0) == lax.broadcasted_iota(jnp.int32, (width, width), 1)
    parts = []
    for f in range(folds):
        row = jnp.broadcast_to(table[f : f + 1, :], (width, width))
        parts.append(jnp.sum(jnp.where(diag, row, 0.0), axis=1, keepdims=True))
    return jnp.concatenate(parts, 0)


def head_tables(head_w, head_b, folds, classes, channels):
    rows, outs = classes * 2 * folds, folds * channels
    lane = lax.broadcasted_iota(jnp.int32, (channels, outs), 1)
    chan = lax.broadcasted_iota(jnp.int32, (channels, outs), 0)
    spread = (lane % channels == chan).astype(F32).astype(BF16)
    tall = []
    for k in range(classes):
        tall += [head_w[k].astype(F32)] * 2
    tall = jnp.concatenate(tall, 0).astype(BF16)
    table = jnp.dot(tall, spread, preferred_element_type=F32)
    row = lax.broadcasted_iota(jnp.int32, (rows, outs), 0)
    col = lax.broadcasted_iota(jnp.int32, (rows, outs), 1)
    table = jnp.where(row % folds == col // channels, table, 0.0).astype(BF16)
    row = lax.broadcasted_iota(jnp.int32, (rows, classes), 0)
    cls = lax.broadcasted_iota(jnp.int32, (rows, classes), 1)
    bias = jnp.zeros((rows, 1), F32)
    for f in range(folds):
        pick = (row // (2 * folds) == cls) & (row % folds == f)
        bias = bias + jnp.sum(jnp.where(pick, jnp.broadcast_to(head_b[f : f + 1, :], (rows, classes)), 0.0), axis=1, keepdims=True)
    return jnp.concatenate([table, table], 1), bias


def gauss(position, length):
    scaled = (position - (length - 1) / 2.0) / (length / 4.0)
    return jnp.exp(-0.5 * scaled * scaled)


def fill_taps(taps, plane, source):
    rows, channels, cols = source.shape
    lane = lax.broadcasted_iota(jnp.int32, (channels, cols), 1)
    not_first = (lane != 0).astype(F32).astype(BF16)
    not_last = (lane != cols - 1).astype(F32).astype(BF16)
    for h in range(rows):
        value = source[h]
        left = pltpu.roll(value, 1, 1) * not_first
        right = pltpu.roll(value, cols - 1, 1) * not_last
        taps[plane, h + 1] = jnp.concatenate([left, value, right], 0)


def run(*steps):
    steps = list(steps)
    while steps:
        for step in list(steps):
            try:
                next(step)
            except StopIteration:
                steps.remove(step)


def conv_plane(x, first, fresh, taps, w_all, conv, stats):
    zero_plane = taps.shape[0] - 1
    cols = taps.shape[-1]
    i = first + x
    below = jnp.where(x == 0, zero_plane, i - 1)
    above = jnp.where(x == PATCH_X - 1, zero_plane, i + 1)
    weights = w_all[...]
    for r in range(PATCH_ROWS // 2):
        halves = []
        for h in (r, r + PATCH_ROWS // 2):
            halves.append(jnp.concatenate([taps[t, h : h + 3].reshape(-1, cols) for t in (below, i, above)], 0))
        out = jnp.dot(weights, jnp.concatenate(halves, 1), preferred_element_type=F32)
        conv[x, r] = out
        one, two = out[:, :cols], out[:, cols:]
        base = stats[0]
        if fresh is not None and r == 0:
            base = jnp.where(fresh, 0.5 * (one + two), base)
            stats[0] = base
        one, two = one - base, two - base
        stats[1] += one + two
        stats[2] += one * one + two * two
        yield


def conv_planes(first, begin, end, fresh, *refs):
    def one_plane(x):
        run(conv_plane(x, first, x == begin if fresh else None, *refs))

    def last_plane(y, _):
        one_plane(end - 1)
        return 0

    def many_planes(y, _):
        for d in range(GROUP):
            one_plane(begin + GROUP * y + d)
        return 0

    total = end - begin
    groups = total // GROUP
    left = lax.rem(total, GROUP)
    lax.fori_loop(0, groups, many_planes, 0)
    begin_left = begin + GROUP * groups

    def two_planes(y, _):
        one_plane(begin_left + 2 * y)
        one_plane(begin_left + 2 * y + 1)
        return 0

    lax.fori_loop(0, left // 2, two_planes, 0)
    lax.fori_loop(0, lax.rem(left, 2), last_plane, 0)


def patch_plan(offs, p, planes):
    even = lax.rem(lax.axis_index("slab"), 2) == 0
    first = RIM - MARGIN + offs[0, p]
    foreign = jnp.where(even, RIM - first, first + PATCH_X - RIM - planes)
    foreign = foreign + jnp.minimum(foreign, 1)
    return even, first, jnp.where(even, foreign, 0), jnp.where(even, PATCH_X, PATCH_X - foreign)


def pre_kernel(offs, own, from_a, wt, gain, nbias, head_w, head_b, taps0, taps1, conv0, conv1, stats0, stats1, w_all, head, hbias, scales):
    planes = own.shape[1]
    classes, folds, channels = head_w.shape
    outs = folds * channels
    cols = own.shape[-1]
    span = planes + 2 * RIM
    even = lax.rem(lax.axis_index("slab"), 2) == 0
    a_base = jnp.where(even, RIM + planes, 0)
    eye = (lax.broadcasted_iota(jnp.int32, (outs, outs), 0) == lax.broadcasted_iota(jnp.int32, (outs, outs), 1)).astype(F32).astype(BF16)
    wide_w = jnp.concatenate([wt[a] for a in range(3)], 0)
    w_all[...] = lax.dot_general(eye, wide_w, (((1,), (1,)), ((), ())), preferred_element_type=F32).astype(BF16)
    table, bias = head_tables(head_w, head_b, folds, classes, channels)
    head[...] = table
    hbias[...] = jnp.broadcast_to(bias, hbias.shape)
    scales[0] = jnp.broadcast_to(column_of(gain, folds, channels), (outs, cols))
    scales[1] = jnp.broadcast_to(column_of(nbias, folds, channels), (outs, cols))
    zero_row = jnp.zeros((3 * channels, cols), BF16)
    for p, taps in enumerate((taps0, taps1)):
        taps[span] = jnp.zeros(taps.shape[1:], BF16)

        def pad_rows(i, _):
            taps[i, 0] = zero_row
            taps[i, PATCH_ROWS + 1] = zero_row
            return 0

        def fill_own(i, _):
            fill_taps(taps, i + RIM, own.at[p, i])
            return 0

        def fill_a(i, _):
            fill_taps(taps, i + a_base, from_a.at[p, i])
            return 0

        lax.fori_loop(0, span, pad_rows, 0)
        lax.fori_loop(0, planes, fill_own, 0, unroll=2)
        lax.fori_loop(0, RIM, fill_a, 0, unroll=2)
    for p, (taps, conv, stats) in enumerate(((taps0, conv0, stats0), (taps1, conv1, stats1))):
        stats[...] = jnp.zeros_like(stats)
        _, first, begin, end = patch_plan(offs, p, planes)
        conv_planes(first, begin, end, True, taps, w_all, conv, stats)


def fill_b(even, from_b, taps):
    planes = taps.shape[0] - 1 - 2 * RIM
    base = jnp.where(even, 0, RIM + planes)

    def fill(i, _):
        fill_taps(taps, i + base, from_b.at[i])
        return 0

    lax.fori_loop(0, RIM, fill, 0, unroll=2)


def settle(stats, scales, norm):
    cols = stats.shape[-1]
    count = float(PATCH_X * PATCH_ROWS)
    total = stats[1] * (1.0 / count)
    spread = stats[2] - total * stats[1]
    lane_mean = stats[0] + total
    mean = jnp.mean(lane_mean, axis=1, keepdims=True)
    dev = lane_mean - mean
    var = jnp.sum(spread + count * dev * dev, axis=1, keepdims=True) * (1.0 / (count * cols))
    scale = lax.rsqrt(var + EPS) * scales[0]
    norm[0] = scale
    norm[1] = scales[1] - mean * scale


def clear_rest(first, placed):
    for q in range(placed.shape[0] - PATCH_X):
        placed[jnp.where(q < first, q, q + PATCH_X)] = jnp.zeros(placed.shape[1:], F32)


def finish_plane(x, first, keep, conv, norm, head, hbias, placed):
    classes, rows, cols = placed.shape[1:]
    folds = rows // 2
    sub = lax.broadcasted_iota(jnp.int32, (rows, cols), 0)
    lane = lax.broadcasted_iota(jnp.int32, (rows, cols), 1)
    lower = sub < folds
    scale, offset = (jnp.concatenate([norm[i], norm[i]], 1) for i in range(2))
    table = [[] for _ in range(classes)]
    for r in range(PATCH_ROWS // 2):
        act = conv[x, r] * scale + offset
        act = jnp.maximum(act, 0.01 * act)
        high = act.astype(BF16)
        low = (act - high.astype(F32)).astype(BF16)
        logits = jnp.dot(head[...], jnp.concatenate([high, low], 0), preferred_element_type=F32) + hbias[...]
        parts = []
        for k in range(classes):
            both = logits[k * rows : (k + 1) * rows]
            parts.append(jnp.where(lower, both[:, :cols], both[:, cols:]))
        top = functools.reduce(jnp.maximum, parts)
        parts = [jnp.exp(v - top) for v in parts]
        denom = 1.0 / functools.reduce(jnp.add, parts)
        for k in range(classes):
            table[k].append(parts[k] * denom)
        yield
    line = gauss(sub.astype(F32), PATCH_ROWS) * gauss(lane.astype(F32), cols)
    window = line * (gauss(jnp.full((rows, cols), x, jnp.int32).astype(F32), PATCH_X) * keep)
    odd = (sub % 2) == 1
    high_pair = (sub % 4) >= 2
    for k in range(classes):
        v = table[k]
        pairs = []
        for q in (0, 2):
            pairs.append(jnp.where(odd, v[q + 1] + pltpu.roll(v[q + 1], 1, 0), v[q] + pltpu.roll(v[q], 7, 0)))
        full = jnp.where(high_pair, pairs[1] + pltpu.roll(pairs[1], 2, 0), pairs[0] + pltpu.roll(pairs[0], 6, 0))
        placed[first + x, k] = full * window


def finish_planes(begin, end, first, keep, *refs):
    def finish(x):
        run(finish_plane(x, first, keep, *refs))

    def many(y, _):
        for d in range(GROUP):
            finish(begin + GROUP * y + d)
        return 0

    def one(x, _):
        finish(x)
        return 0

    groups = (end - begin) // GROUP
    lax.fori_loop(0, groups, many, 0)
    lax.fori_loop(begin + GROUP * groups, end, one, 0)


def mid_kernel(offs, mask, from_b, taps_in, conv_in, stats_in, w_all, head, hbias, scales, placed, norm, taps, conv, stats):
    planes = taps.shape[0] - 1 - 2 * RIM
    folds = placed.shape[2] // 2
    even, first, begin, end = patch_plan(offs, 0, planes)
    fill_b(even, from_b, taps)
    conv_planes(first, jnp.where(even, 0, end), jnp.where(even, begin, PATCH_X), False, taps, w_all, conv, stats)
    settle(stats, scales, norm)
    clear_rest(first, placed)
    _, _, begin, end = patch_plan(offs, 1, planes)
    finish_planes(0, end - begin, first, mask[0, 0].astype(F32) * (1.0 / folds), conv, norm, head, hbias, placed)


def post_kernel(offs, mask, from_b, conv0, norm0, w_all, head, hbias, scales, taps_in, conv_in, stats_in, placed0_in, placed0, placed1, to_a, to_b, taps, conv, stats, norm1):
    planes = taps.shape[0] - 1 - 2 * RIM
    folds = placed1.shape[2] // 2
    even, first0, _, _ = patch_plan(offs, 0, planes)
    _, first1, begin, end = patch_plan(offs, 1, planes)
    fill_b(even, from_b, taps)
    keep0, keep1 = (mask[0, p].astype(F32) * (1.0 / folds) for p in range(PATCHES))
    done = end - begin
    waiting = jnp.where(even, 0, end)

    def both(y, _):
        run(conv_plane(waiting + y, first1, None, taps, w_all, conv, stats), finish_plane(done + y, first0, keep0, conv0, norm0, head, hbias, placed0))
        return 0

    def both_twice(y, _):
        both(2 * y, 0)
        both(2 * y + 1, 0)
        return 0

    left = PATCH_X - done
    lax.fori_loop(0, left // 2, both_twice, 0)
    lax.fori_loop(left // 2 * 2, left, both, 0)
    settle(stats, scales, norm1)
    clear_rest(first1, placed1)
    finish_planes(0, PATCH_X, first1, keep1, conv, norm1, head, hbias, placed1)
    for send, begin in ((to_a, jnp.where(even, planes + RIM - 1, 0)), (to_b, jnp.where(even, 0, planes + RIM - 1))):
        for p, placed in enumerate((placed0, placed1)):
            for j in range(RIM + 1):
                send[p, j] = (placed[begin + j] * UNIT + 0.5).astype(jnp.int32).astype(jnp.int16)


def gather_kernel(placed0, placed1, from_a, summed):
    planes = placed0.shape[0] - 2 * RIM
    wide = planes + 2
    even = lax.rem(lax.axis_index("slab"), 2) == 0
    base = jnp.where(even, wide - RIM - 1, 0)
    for p, placed in enumerate((placed0, placed1)):
        summed[p] = placed[RIM - 1 : RIM - 1 + wide]
        for j in range(RIM + 1):
            summed[p, base + j] += from_a[p, j].astype(jnp.int32).astype(F32) * (1.0 / UNIT)


def merge_kernel(slabs, acq, summed, from_b, out, merged, held, sems):
    wide = summed.shape[1]
    planes = wide - 2
    classes, rows, cols = summed.shape[2:]
    slab = lax.axis_index("slab")
    even = lax.rem(slab, 2) == 0
    base = jnp.where(even, 0, wide - RIM - 1)
    shape = (rows, cols)
    gaps = jnp.maximum(acq[0] - 1, 1)
    count = jnp.full(shape, acq[0], jnp.int32).astype(F32)
    anchor = jnp.full(shape, slab * planes, jnp.int32).astype(F32)
    step = planes / jnp.maximum(count - 1.0, 1.0)
    lowest = jnp.where(slab == 0, 0, -1)
    firsts, gains = [], []
    for s in range(MOST_ACQ):
        first = lax.div(2 * planes * s + gaps, 2 * gaps) - 1
        first = jnp.minimum(jnp.maximum(first, lowest), planes - 1)
        place = jnp.clip(anchor + (s * step - 0.5), 0.0, float(slabs * planes - 1)) - anchor
        used = (s < count).astype(F32)
        near = place - jnp.full(shape, first, jnp.int32).astype(F32)
        firsts.append(first + 1)
        gains.append([jnp.maximum(0.0, 1.0 - jnp.abs(near - d)) * used for d in range(2)])
    for p in range(PATCHES):
        merged[p] = summed[p]
        for j in range(RIM + 1):
            merged[p, base + j] += from_b[p, j].astype(jnp.int32).astype(F32) * (1.0 / UNIT)
        for j in range(wide):
            parts = [merged[p, j, k] for k in range(classes)]
            scale = 1.0 / (functools.reduce(jnp.add, parts) + PRIOR)
            parts[0] = parts[0] + PRIOR
            for k in range(classes):
                merged[p, j, k] = parts[k] * scale
    copies = []
    for k in range(classes):
        for p in range(PATCHES):
            for s in range(MOST_ACQ):
                held[k, s, p * rows : (p + 1) * rows] = gains[s][0] * merged[p, firsts[s], k] + gains[s][1] * merged[p, firsts[s] + 1, k]
        copies.append(pltpu.make_async_copy(held.at[k], out.at[k], sems.at[k]))
        copies[-1].start()
    for copy in copies:
        copy.wait()


def local(slabs, features, conv_weight, norm_gain, norm_bias, head_weight, head_bias, patch_offsets, fg_mask, acq_counts):
    channels, planes, row_total, cols = features.shape
    folds, classes, _ = head_weight.shape
    outs = folds * channels
    pairs_a = [(i, i ^ 1) for i in range(slabs) if (i ^ 1) < slabs]
    pairs_b = [(i, ((i + 1) ^ 1) - 1) for i in range(slabs) if 0 <= ((i + 1) ^ 1) - 1 < slabs]
    shaped = jax.ShapeDtypeStruct
    cell = (PATCH_ROWS, channels, cols)
    halo_shape = shaped((RIM,) + cell, BF16)
    params = pltpu.CompilerParams(vmem_limit_bytes=24 * MIB)
    small = [jnp.swapaxes(conv_weight, 1, 2), norm_gain, norm_bias, jnp.swapaxes(head_weight, 0, 1), head_bias, patch_offsets, fg_mask]
    own, to_a, *rest = pl.pallas_call(
        prep_kernel,
        out_shape=[shaped((PATCHES, planes) + cell, BF16), shaped((PATCHES, RIM) + cell, BF16)]
        + [halo_shape] * PATCHES
        + [shaped(v.shape, v.dtype) for v in small],
        in_specs=[pl.BlockSpec(memory_space=pltpu.HBM)] * (1 + len(small)),
        out_specs=[vmem()] * (2 + PATCHES + len(small)),
        scratch_shapes=[pltpu.VMEM((planes, channels, row_total, cols), BF16), pltpu.SemaphoreType.DMA((planes + len(small),))],
        compiler_params=params,
        name="prep",
    )(*[pltpu.with_memory_space_constraint(v, pltpu.HBM) for v in (features, *small)])
    to_b, (conv_weight, norm_gain, norm_bias, head_weight, head_bias, patch_offsets, fg_mask) = rest[:PATCHES], rest[PATCHES:]
    from_a = lax.ppermute(to_a, "slab", pairs_a)
    from_b = [lax.ppermute(v, "slab", pairs_b) for v in to_b]
    wide = planes + 2
    tile = (classes, PATCH_ROWS, cols)
    span = planes + 2 * RIM
    taps_shape = shaped((span + 1, PATCH_ROWS + 2, 3 * channels, cols), BF16)
    conv_shape = shaped((PATCH_X, PATCH_ROWS // 2, outs, 2 * cols), F32)
    stats_shape = shaped((3, outs, cols), F32)
    table_shapes = [shaped((outs, 27 * channels), BF16), shaped((classes * 2 * folds, 2 * outs), BF16), shaped((classes * 2 * folds, 2 * cols), F32), shaped((2, outs, cols), F32)]
    placed_shape = shaped((span,) + tile, F32)
    norm_shape = shaped((2, outs, cols), F32)
    send_shape = shaped((PATCHES, RIM + 1) + tile, jnp.int16)
    taps0, taps1, conv0, conv1, stats0, stats1, *tables = pl.pallas_call(
        pre_kernel,
        out_shape=[taps_shape] * 2 + [conv_shape] * 2 + [stats_shape] * 2 + table_shapes,
        in_specs=[smem()] + [vmem()] * 7,
        out_specs=[vmem()] * 10,
        compiler_params=params,
        name="pre",
    )(patch_offsets, own, from_a, conv_weight, norm_gain, norm_bias, head_weight, head_bias)
    placed0, norm0, _, conv0, _ = pl.pallas_call(
        mid_kernel,
        out_shape=[placed_shape, norm_shape, taps_shape, conv_shape, stats_shape],
        in_specs=[smem()] * 2 + [vmem()] * 8,
        out_specs=[vmem()] * 5,
        input_output_aliases={3: 2, 4: 3, 5: 4},
        compiler_params=params,
        name="mid",
    )(patch_offsets, fg_mask, from_b[0], taps0, conv0, stats0, *tables)
    placed0, placed1, send_a, send_b, *_ = pl.pallas_call(
        post_kernel,
        out_shape=[placed_shape, placed_shape, send_shape, send_shape, taps_shape, conv_shape, stats_shape],
        in_specs=[smem()] * 2 + [vmem()] * 11,
        out_specs=[vmem()] * 7,
        input_output_aliases={12: 0, 9: 4, 10: 5, 11: 6},
        scratch_shapes=[pltpu.VMEM(norm_shape.shape, F32)],
        compiler_params=params,
        name="post",
    )(patch_offsets, fg_mask, from_b[1], conv0, norm0, *tables, taps1, conv1, stats1, placed0)
    got_a = lax.ppermute(send_a, "slab", pairs_a)
    got_b = lax.ppermute(send_b, "slab", pairs_b)
    summed = pl.pallas_call(
        gather_kernel,
        out_shape=shaped((PATCHES, wide) + tile, F32),
        in_specs=[vmem()] * 3,
        out_specs=vmem(),
        compiler_params=params,
        name="gather",
    )(placed0, placed1, got_a)
    return pl.pallas_call(
        functools.partial(merge_kernel, slabs),
        out_shape=shaped((classes, MOST_ACQ, row_total, cols), F32),
        in_specs=[smem()] + [vmem()] * 2,
        out_specs=pl.BlockSpec(memory_space=pltpu.HBM),
        scratch_shapes=[
            pltpu.VMEM((PATCHES, wide) + tile, F32),
            pltpu.VMEM((classes, MOST_ACQ, row_total, cols), F32),
            pltpu.SemaphoreType.DMA((classes,)),
        ],
        compiler_params=params,
        name="merge",
    )(acq_counts, summed, got_b)


def solution(mesh):
    part = ("brain", "slab")
    in_specs = (P(None, part, None, None), P(), P(), P(), P(), P(), P(part, None), P(part, None), P(part))
    body = functools.partial(local, mesh.shape["slab"])
    return jax.shard_map(body, mesh=mesh, in_specs=in_specs, out_specs=P(None, part, None, None), check_vma=False)
```
